768 devices in a mesh: member: 8 (over y), domain: 12 (over z), role: 8 (over x, core).
Axes of the slice: x: 4, y: 8, z: 12, core: 2. Of those that a mesh axis runs over, the one named last changes fastest.
Arguments:
- ensemble: float32 [256, 768, 1024], P('member', 'domain', 'role'), may hold values from -6 to 6
- diffusion: float32 [768, 1024], P('domain', 'role'), may hold values from 0.02 to 0.1
- drift_rows: float32 [768, 1024], P('domain', 'role'), may hold values from 0.05 to 0.3
- drift_cols: float32 [768, 1024], P('domain', 'role'), may hold values from 0.05 to 0.3
- observed_cells: int32 [12, 1024], P('domain'), may hold values from 0 to 65535
- observed_count: int32 [12], P('domain'), may hold values from 256 to 1024
- observed_values: float32 [12, 1024], P('domain'), may hold values from -6 to 6
- observed_weights: float32 [12, 1024], P('domain'), may hold values from 0.5 to 4
Outputs:
- analysis: float32 [256, 768, 1024], P('member', 'domain', 'role')
The draws below stay inside these ranges and needn't reach their ends.
All inputs are finite; a program needn't handle non-finite values.
Results may differ from the reference program's by a relative error of at most 0.0003.
Values sent between devices are 32-bit elements; how exact they have to be, the bound alone decides.
A program may use at most 64 MiB of HBM per device.

```python
import math
import jax
import jax.numpy as jnp
import numpy as np
from jax import lax

ENSEMBLE_SIZE = 256
OBS_REG = 1024
STEPS = 4
ITERS = 6
CX = 64
REGIONS = 12
GRID_ROWS = 768
GRID_COLUMNS = 1024
N_MEMBER = 8


def place_ends(array, own_key, smallest, top_value):
    shape = array.shape
    spot = [jax.random.randint(jax.random.fold_in(own_key, axis), (), 0, shape[axis]) for axis in range(len(shape))]
    array = array.at[tuple(spot)].set(smallest)
    longest = shape.index(max(shape))
    spot[longest] = (spot[longest] + 1) % shape[longest]
    return array.at[tuple(spot)].set(top_value)


def shard_levels(own_key, shape, pieces, least, top_value):
    level = 1.0
    for dim, blocks in pieces:
        heights = jax.random.uniform(jax.random.fold_in(jax.random.fold_in(own_key, 6), dim), (blocks,), jnp.float32, least / len(pieces), top_value / len(pieces))
        level = level * jnp.repeat(jnp.exp(heights), shape[dim] // blocks).reshape((-1,) + (1,) * (len(shape) - 1 - dim))
    return level


def rank_table(amount, skew):
    weights = [(1 << 20) // math.isqrt(grade ** skew) + 1 for grade in range(1, amount + 1)]
    scale = 1 + sum(weights) // (1 << 30)
    return np.cumsum(np.array([max(1, weight // scale) for weight in weights]))


def ranked_ids(own_key, shape, amount, lean):
    grid = rank_table(amount, lean)
    lot = jax.random.randint(jax.random.fold_in(own_key, 1), shape, 0, int(grid[amount - 1]))
    grade = jnp.searchsorted(jnp.asarray(grid, jnp.int32), lot, side="right")
    return jax.random.permutation(jax.random.fold_in(own_key, 2), amount)[grade].astype(jnp.int32)


def centred(rng, shape, scale, most, cuts=(), kind=jnp.bfloat16):
    loudness = shard_levels(rng, shape, cuts, -0.22, 0.18) if cuts else 1.0
    values = jax.random.normal(rng, shape, jnp.float32) * scale * loudness
    return jnp.minimum(jnp.maximum(values, -most), most).astype(kind)


def setup_inputs(seed: int = 0) -> dict:
    keys = jax.random.split(jax.random.key(seed), 9)
    ensemble = centred(keys[0], (ENSEMBLE_SIZE, GRID_ROWS, GRID_COLUMNS), 1.0, 6.0, ((0, 8), (1, 12), (2, 8)), jnp.float32)
    diffusion = jnp.clip(0.02 + 0.08 * jax.random.uniform(keys[1], (GRID_ROWS, GRID_COLUMNS), jnp.float32) ** shard_levels(keys[1], (GRID_ROWS, GRID_COLUMNS), ((0, 12), (1, 8)), -0.2, 0.2), 0.02, 0.1)
    drift_rows = jnp.clip(0.05 + 0.25 * jax.random.uniform(keys[2], (GRID_ROWS, GRID_COLUMNS), jnp.float32) ** shard_levels(keys[2], (GRID_ROWS, GRID_COLUMNS), ((0, 12), (1, 8)), -0.2, 0.2), 0.05, 0.3)
    drift_cols = jnp.clip(0.05 + 0.25 * jax.random.uniform(keys[3], (GRID_ROWS, GRID_COLUMNS), jnp.float32) ** shard_levels(keys[3], (GRID_ROWS, GRID_COLUMNS), ((0, 12), (1, 8)), -0.2, 0.2), 0.05, 0.3)
    observed_cells = place_ends(ranked_ids(keys[4], (REGIONS, OBS_REG), CX * GRID_COLUMNS, 2), jax.random.fold_in(keys[4], 3), 0, (CX * GRID_COLUMNS) - 1).astype(jnp.int32)
    observed_count = place_ends(jax.random.randint(keys[5], (REGIONS,), OBS_REG // 4, OBS_REG + 1), jax.random.fold_in(keys[5], 1), OBS_REG // 4, OBS_REG).astype(jnp.int32)
    observed_values = centred(keys[6], (REGIONS, OBS_REG), 1.0, 6.0, ((0, 12),), jnp.float32)
    observed_weights = jnp.clip(jnp.exp(math.log(4.0) - 2.0794415 * jax.random.uniform(keys[7], (REGIONS, OBS_REG), jnp.float32) ** shard_levels(keys[7], (REGIONS, OBS_REG), ((0, 12),), -0.2, 0.2)), 0.5, 4.0)
    return {"ensemble": ensemble, "diffusion": diffusion, "drift_rows": drift_rows, "drift_cols": drift_cols, "observed_cells": observed_cells, "observed_count": observed_count, "observed_values": observed_values, "observed_weights": observed_weights}


precise = lax.Precision.HIGHEST

def advance(values, diffusion, drift_rows, drift_cols):
    ahead_rows = jnp.roll(values, -1, 1)
    behind_rows = jnp.roll(values, 1, 1)
    ahead_cols = jnp.roll(values, -1, 2)
    behind_cols = jnp.roll(values, 1, 2)
    spread = ahead_rows + behind_rows + ahead_cols + behind_cols - 4.0 * values
    return values + diffusion * spread - drift_rows * (values - behind_rows) - drift_cols * (values - behind_cols)

def inverse_root(matrix):
    extent = matrix.shape[0]
    identity = jnp.eye(extent, dtype=jnp.float32)
    scaling = jnp.sqrt(jnp.sum(matrix * matrix))
    current = matrix / scaling
    inverse = identity
    for repeat in range(ITERS):
        middle = 0.5 * (3.0 * identity - jnp.dot(inverse, current, precision=precise))
        current = jnp.dot(current, middle, precision=precise)
        inverse = jnp.dot(middle, inverse, precision=precise)
    return (inverse, scaling)

def analysis_weights(gram_sum, innovation):
    extent = gram_sum.shape[0]
    matrix = gram_sum + (extent - 1.0) * jnp.eye(extent, dtype=jnp.float32)
    inverse, scaling = inverse_root(matrix)
    spread = jnp.sqrt((extent - 1.0) / scaling) * inverse
    shifted = jnp.dot(inverse, jnp.dot(inverse, innovation, precision=precise), precision=precise) / scaling
    return spread + shifted[:, None]

def stripe_analysis(stripe, cell_index, counts, values, weights):
    flattened = stripe.reshape(stripe.shape[0], -1)
    observed = jnp.take(flattened, cell_index, axis=1)
    centre_obs = lax.optimization_barrier(jnp.mean(observed, axis=0))
    deviation = observed - centre_obs
    usable = jnp.arange(cell_index.shape[0]) < counts
    weighted = deviation * jnp.where(usable, weights, jnp.float32(0.0))
    gram_sum = jnp.dot(weighted, deviation.T, precision=precise)
    innovation = jnp.dot(weighted, values - centre_obs, precision=precise)
    mixing = analysis_weights(gram_sum, innovation)
    centre = lax.optimization_barrier(jnp.mean(flattened, axis=0))
    updated = centre + jnp.dot(mixing.T, flattened - centre, precision=precise)
    return updated.reshape(stripe.shape)

def reference(ensemble, diffusion, drift_rows, drift_cols, observed_cells, observed_count, observed_values, observed_weights):
    partition_sets = ensemble.reshape(N_MEMBER, ENSEMBLE_SIZE // N_MEMBER, GRID_ROWS, GRID_COLUMNS)

    def predicted_fields(ensemble_states):
        for repeat in range(STEPS):
            ensemble_states = advance(ensemble_states, diffusion, drift_rows, drift_cols)
        return ensemble_states
    stepped_forward = lax.map(predicted_fields, partition_sets).reshape(ENSEMBLE_SIZE, GRID_ROWS, GRID_COLUMNS)

    def analyse(region):
        stripe = lax.dynamic_slice_in_dim(stepped_forward, (region * CX).astype(jnp.int32), CX, 1)
        return stripe_analysis(stripe, observed_cells[region], observed_count[region], observed_values[region], observed_weights[region])
    result = lax.map(analyse, jnp.arange(REGIONS, dtype=jnp.int32))
    return jnp.transpose(result, (1, 0, 2, 3)).reshape(ENSEMBLE_SIZE, GRID_ROWS, GRID_COLUMNS)
```

```python
import functools

import jax
import jax.numpy as jnp
from jax import lax
from jax.experimental import pallas as pl
from jax.experimental.pallas import tpu as pltpu
from jax.sharding import PartitionSpec as P

STEPS = 4
ITERS = 6
LANES = 128
GROUP = 8
SEG = 24
F32 = jnp.float32
BF16 = jnp.bfloat16
MESH = pl.DeviceIdType.MESH
NN = (((1,), (0,)), ((), ()))
NT = (((1,), (1,)), ((), ()))


def halves(a):
    high = a.astype(BF16)
    return high, (a - high.astype(F32)).astype(BF16)


def product(a, b, dims=NN):
    (ah, al), (bh, bl) = a, b
    dot = functools.partial(lax.dot_general, dimension_numbers=dims, preferred_element_type=F32)
    return dot(ah, bh) + (dot(ah, bl) + dot(al, bh))


def kernel(
    sizes,
    count_ref,
    fields_ref,
    cells_ref,
    values_ref,
    weights_ref,
    out_ref,
    field_a,
    field_b,
    strip_a,
    strip_b,
    strip_coef,
    pack_right,
    pack_left,
    halo_left,
    halo_right,
    final,
    received,
    obs_part,
    obs_role,
    obs_own,
    obs_all,
    gram_part,
    gram_role,
    gram_own,
    gram,
    current,
    inverse,
    mixing,
    dev_high,
    dev_low,
    centre_buf,
    result,
    load_sem,
    halo_send,
    halo_recv,
    peer_send,
    peer_recv,
):
    n_member, n_domain, n_role, members = sizes
    rows = 64
    chunk = rows // n_member
    total = members * n_member
    slot_groups = 8 // n_role
    gram_rows = total // n_role
    groups = members // GROUP
    me_m = lax.axis_index("member")
    me_d = lax.axis_index("domain")
    me_r = lax.axis_index("role")

    def other(me, step, n):
        return lax.rem(me + (step + n), n)

    down, up = other(me_d, 1, n_domain), other(me_d, -1, n_domain)
    right, left = other(me_r, 1, n_role), other(me_r, -1, n_role)

    load = pltpu.make_async_copy(fields_ref, field_a.at[4 : 4 + rows], load_sem.at[0])
    load.start()

    barrier = pltpu.get_barrier_semaphore()
    greeted = 0
    for d in (down, up):
        for r in (me_r, right, left):
            pl.semaphore_signal(barrier, inc=1, device_id={"domain": d, "role": r}, device_id_type=MESH)
            greeted += 1
    for step in range(1, n_role):
        pl.semaphore_signal(barrier, inc=1, device_id={"role": other(me_r, step, n_role)}, device_id_type=MESH)
        greeted += 1
    for step in range(1, n_member):
        pl.semaphore_signal(barrier, inc=1, device_id={"member": other(me_m, step, n_member)}, device_id_type=MESH)
        greeted += 1

    lane = lax.broadcasted_iota(jnp.int32, (GROUP, LANES), 1)
    seg_lane = lane
    for s in range(1, 6):
        seg_lane = jnp.where(lane >= SEG * s, lane - SEG * s, seg_lane)

    def own_strip(row):
        strip = jnp.zeros((GROUP, LANES), F32)
        for s in range(groups + 1):
            block = field_a[row, GROUP * s : GROUP * (s + 1), :]
            base = SEG * s
            ends = pltpu.roll(block, (base + 8) % LANES, 1)
            starts = pltpu.roll(block, (base + 16) % LANES, 1)
            strip = jnp.where((lane >= base) & (lane < base + 8), ends, strip)
            strip = jnp.where((lane >= base + 16) & (lane < base + 24), starts, strip)
        return strip

    load.wait()

    def pack(q, carry):
        to_right = to_left = jnp.zeros((GROUP, LANES), F32)
        for t in range(4):
            row = 4 + 4 * q + t
            strip = own_strip(row)
            strip_a[row] = strip
            low, high = 4 + 4 * t, 16 - 4 * t
            moved = pltpu.roll(strip, 4 * t, 1) if t else strip
            to_right = jnp.where((seg_lane >= low) & (seg_lane < low + 4), moved, to_right)
            moved = pltpu.roll(strip, LANES - 4 * t, 1) if t else strip
            to_left = jnp.where((seg_lane >= high) & (seg_lane < high + 4), moved, to_left)
        pack_right[q] = to_right
        pack_left[q] = to_left
        return carry

    pl.semaphore_wait(barrier, greeted)

    def halo_copy(k, src, dst, where):
        return pltpu.make_async_remote_copy(
            src_ref=src, dst_ref=dst, send_sem=halo_send.at[k], recv_sem=halo_recv.at[k],
            device_id=where, device_id_type=MESH,
        )

    quads = rows // 4
    row_halos = [
        halo_copy(0, fields_ref.at[rows - 4 : rows], field_a.at[0:4], {"domain": down}),
        halo_copy(1, fields_ref.at[0:4], field_a.at[rows + 4 : rows + 8], {"domain": up}),
    ]
    for copy in row_halos:
        copy.start()
    lax.fori_loop(0, quads, pack, 0, unroll=2)
    col_halos = [
        halo_copy(4, pack_right.at[quads - 1], halo_left.at[0], {"domain": down, "role": right}),
        halo_copy(5, pack_right.at[0], halo_left.at[quads + 1], {"domain": up, "role": right}),
        halo_copy(6, pack_left.at[quads - 1], halo_right.at[0], {"domain": down, "role": left}),
        halo_copy(7, pack_left.at[0], halo_right.at[quads + 1], {"domain": up, "role": left}),
        halo_copy(2, pack_right, halo_left.at[1 : quads + 1], {"role": right}),
        halo_copy(3, pack_left, halo_right.at[1 : quads + 1], {"role": left}),
    ]
    for copy in col_halos:
        copy.start()
    for copy in row_halos:
        copy.wait()
    for t in range(4):
        strip_a[t] = own_strip(t)
        strip_a[rows + 4 + t] = own_strip(rows + 4 + t)
    for copy in col_halos:
        copy.wait()

    def unpack(q, carry):
        from_left = halo_left[q]
        from_right = halo_right[q]
        for t in range(4):
            row = 4 * q + t
            strip = strip_a[row]
            moved = pltpu.roll(from_left, (8 - 4 * t) % LANES, 1) if t != 2 else from_left
            strip = jnp.where((seg_lane >= 12) & (seg_lane < 16), moved, strip)
            moved = pltpu.roll(from_right, (4 * t - 8) % LANES, 1) if t != 2 else from_right
            strip = jnp.where((seg_lane >= 8) & (seg_lane < 12), moved, strip)
            strip_a[row] = strip
            coef = strip
            for s in range(groups):
                moved = pltpu.roll(strip, (SEG * (s - groups)) % LANES, 1)
                coef = jnp.where((lane >= SEG * s) & (lane < SEG * (s + 1)), moved, coef)
            strip_coef[row] = coef
        return carry

    lax.fori_loop(0, quads + 2, unpack, 0, unroll=2)

    def advanced(now, before, after, coef):
        return (
            now * coef[0]
            + (after + pltpu.roll(now, LANES - 1, 1)) * coef[1]
            + before * coef[2]
            + pltpu.roll(now, 1, 1) * coef[3]
        )

    def field_coef(row):
        return [field_a[row, members + k : members + k + 1, :] for k in range(4)]

    def seam_coef(row):
        return [strip_coef[row, k : k + 1, :] for k in range(4)]

    def step_rows(source, target, strip_source, strip_target, first, amount):
        before = source[first - 1, :members, :]
        now = source[first, :members, :]
        seam_before = strip_source[first - 1]
        seam_now = strip_source[first]
        for i in range(amount):
            row = first + i
            after = source[row + 1, :members, :]
            seam_after = strip_source[row + 1]
            target[row, :members, :] = advanced(now, before, after, field_coef(row))
            strip_target[row] = advanced(seam_now, seam_before, seam_after, seam_coef(row))
            before, now = now, after
            seam_before, seam_now = seam_now, seam_after

    pairs = ((field_a, field_b, strip_a, strip_b), (field_b, field_a, strip_b, strip_a))
    for step in range(STEPS - 1):

        def body(i, carry, refs=pairs[step % 2]):
            step_rows(*refs, 1 + 10 * i, 10)
            return carry

        lax.fori_loop(0, 7, body, 0)

    source, _, strip_source, _ = pairs[(STEPS - 1) % 2]

    def last_rows(first, amount):
        before = source[first - 1, :members, :]
        now = source[first, :members, :]
        seam_before = strip_source[first - 1]
        seam_now = strip_source[first]
        for i in range(amount):
            row = first + i
            after = source[row + 1, :members, :]
            seam_after = strip_source[row + 1]
            new = advanced(now, before, after, field_coef(row))
            seam = advanced(seam_now, seam_before, seam_after, seam_coef(row))
            for s in range(groups):
                begin = pltpu.roll(seam, (-(SEG * s + 16)) % LANES, 1)
                end = pltpu.roll(seam, (120 - SEG * s) % LANES, 1)
                block = new[GROUP * s : GROUP * (s + 1), :]
                block = jnp.where(lane < 4, begin, jnp.where(lane >= LANES - 4, end, block))
                final[row - 4, GROUP * s : GROUP * (s + 1), :] = block
            before, now = now, after
            seam_before, seam_now = seam_now, seam_after

    def last_body(i, carry):
        last_rows(4 + 8 * i, 8)
        return carry

    lax.fori_loop(0, rows // 8, last_body, 0)

    def peer_copy(stage, step, src, dst, axis):
        me, n = (me_m, n_member) if axis == "member" else (me_r, n_role)
        return pltpu.make_async_remote_copy(
            src_ref=src, dst_ref=dst, send_sem=peer_send.at[stage, step], recv_sem=peer_recv.at[stage, step],
            device_id={axis: other(me, step, n)}, device_id_type=MESH,
        )

    order = sorted(range(1, n_member), key=lambda s: -min(s, n_member - s))
    forward = []
    for step in order:
        first = pl.multiple_of(chunk * other(me_m, step, n_member), chunk)
        forward.append(
            peer_copy(
                0, step, final.at[pl.ds(first, chunk)],
                received.at[:, pl.ds(pl.multiple_of(members * me_m, members), members), :], "member",
            )
        )
    keep = pltpu.make_async_copy(
        final.at[pl.ds(pl.multiple_of(chunk * me_m, chunk), chunk)],
        received.at[:, pl.ds(pl.multiple_of(members * me_m, members), members), :],
        load_sem.at[1],
    )
    early = 2
    for copy in forward[:early]:
        copy.start()

    def observe(g, carry):
        cell = cells_ref[pl.ds(g, 1), :]
        here = ((cell // LANES) % n_role) == me_r
        row_of = jnp.where(here, cell // (LANES * n_role), -1)
        row_of = jnp.broadcast_to(row_of, (members, LANES))
        col_of = jnp.broadcast_to(cell % LANES, (members, LANES))

        def some(q, seen):
            for t in range(16):
                row = 16 * q + t
                picked = jnp.take_along_axis(final[row], col_of, axis=1, mode="promise_in_bounds")
                seen = jnp.where(row_of == row, picked, seen)
            return seen

        obs_part[g] = lax.fori_loop(0, rows // 16, some, jnp.zeros((members, LANES), F32))
        return carry

    lax.fori_loop(0, 8, observe, 0)

    def own_groups(r):
        return pl.ds(slot_groups * r, slot_groups)

    copies = []
    for step in range(1, n_role):
        copies.append(
            peer_copy(1, step, obs_part.at[own_groups(other(me_r, step, n_role))], obs_role.at[me_r], "role")
        )
        copies[-1].start()
    obs_role[me_r] = obs_part[own_groups(me_r)]
    for copy in copies:
        copy.wait()
    obs_own[...] = functools.reduce(jnp.add, [obs_role[r] for r in range(n_role)])

    mine = pl.ds(pl.multiple_of(members * me_m, members), members)
    copies = []
    for step in order:
        copies.append(peer_copy(2, step, obs_own, obs_all.at[:, mine, :], "member"))
        copies[-1].start()
    for copy in forward[early:]:
        copy.start()
    keep.start()
    obs_all[:, mine, :] = obs_own[...]
    for copy in copies:
        copy.wait()

    part = jnp.zeros((total, total), F32)
    push = jnp.zeros((GROUP, total), F32)
    slot = lax.broadcasted_iota(jnp.int32, (1, LANES), 1)
    for g in range(slot_groups):
        place = slot_groups * me_r + g
        observed = obs_all[g]
        centre = jnp.sum(observed, axis=0, keepdims=True) * (1.0 / total)
        deviation = observed - centre
        usable = slot + place * LANES < count_ref[0]
        weighted = deviation * jnp.where(usable, weights_ref[pl.ds(place, 1), :], 0.0)
        gap = jnp.broadcast_to(values_ref[pl.ds(place, 1), :] - centre, (GROUP, LANES))
        weighted = halves(weighted)
        part = part + product(halves(deviation), weighted, NT)
        push = push + product(halves(gap), weighted, NT)
    for r in range(n_role):
        gram_part[r, :gram_rows, :] = part[gram_rows * r : gram_rows * (r + 1), :]
        gram_part[r, gram_rows:, :] = push

    copies = []
    for step in range(1, n_role):
        copies.append(
            peer_copy(3, step, gram_part.at[other(me_r, step, n_role)], gram_role.at[me_r], "role")
        )
        copies[-1].start()
    gram_role[me_r] = gram_part[me_r]
    for copy in copies:
        copy.wait()
    summed = functools.reduce(jnp.add, [gram_role[r] for r in range(n_role)])
    innovation = summed[gram_rows:, :]
    gram_own[...] = summed[:gram_rows, :]
    band = pl.ds(pl.multiple_of(gram_rows * me_r, gram_rows), gram_rows)
    copies = []
    for step in range(1, n_role):
        copies.append(peer_copy(4, step, gram_own, gram.at[band, :], "role"))
        copies[-1].start()
    gram[band, :] = gram_own[...]
    for copy in copies:
        copy.wait()

    across = lax.broadcasted_iota(jnp.int32, (total, total), 1)
    along = lax.broadcasted_iota(jnp.int32, (total, total), 0)
    diagonal = across == along
    matrix = gram[...] + jnp.where(diagonal, total - 1.0, 0.0)
    squares = jnp.sum(jnp.sum(matrix * matrix, axis=0, keepdims=True), axis=1, keepdims=True)
    scaling = jnp.sqrt(squares)
    scaled = matrix / scaling
    middle = jnp.where(diagonal, 1.5, 0.0) - 0.5 * scaled
    current[...] = product(halves(scaled), halves(middle))
    inverse[...] = middle

    def newton(i, carry):
        cur, inv = halves(current[...]), halves(inverse[...])
        mid = halves(jnp.where(diagonal, 1.5, 0.0) - 0.5 * product(inv, cur))
        current[...] = product(cur, mid)
        inverse[...] = product(mid, inv)
        return carry

    lax.fori_loop(0, ITERS - 2, newton, 0)
    inv = halves(inverse[...])
    mid = halves(jnp.where(diagonal, 1.5, 0.0) - 0.5 * product(inv, halves(current[...])))
    root = product(mid, inv)
    root_halves = halves(root)
    shifted = product(halves(product(halves(innovation), root_halves)), root_halves) / scaling
    mixing[...] = root * jnp.sqrt((total - 1.0) / scaling) + shifted[0:1, :]

    for copy in forward:
        copy.wait()
    keep.wait()
    for i in range(chunk):
        block = received[i]
        centre = jnp.sum(block, axis=0, keepdims=True) * (1.0 / total)
        high, low = halves(block - centre)
        span = slice(LANES * i, LANES * (i + 1))
        dev_high[:, span] = high
        dev_low[:, span] = low
        centre_buf[:, span] = centre

    back = []
    target_rows = pl.ds(pl.multiple_of(chunk * me_m, chunk), chunk)
    for step in order + [0]:
        first = pl.multiple_of(members * other(me_m, step, n_member), members)
        share = halves(mixing[pl.ds(first, members), :])
        updated = product(share, (dev_high[...], dev_low[...])) + centre_buf[...]
        for i in range(chunk):
            result[step, i] = updated[:, LANES * i : LANES * (i + 1)]
        if step:
            copy = peer_copy(5, step, result.at[step], out_ref.at[target_rows], "member")
        else:
            copy = pltpu.make_async_copy(result.at[step], out_ref.at[target_rows], load_sem.at[2])
        copy.start()
        back.append(copy)
    for copy in back:
        copy.wait()


def shards(sizes, ensemble, diffusion, drift_rows, drift_cols, cells, count, values, weights):
    n_member, n_domain, n_role = sizes
    members, rows, cols = ensemble.shape
    total = members * n_member
    coef = jnp.stack(
        [
            1.0 - 4.0 * diffusion - drift_rows - drift_cols,
            diffusion,
            diffusion + drift_rows,
            diffusion + drift_cols,
        ]
        + [jnp.zeros_like(diffusion)] * 4,
        axis=1,
    )
    fields = jnp.concatenate([jnp.transpose(ensemble, (1, 0, 2)), coef], axis=1)
    planes = members + GROUP
    chunk = rows // n_member
    slot_groups = 8 // n_role
    gram_rows = total // n_role

    def vmem(*shape, dtype=F32):
        return pltpu.VMEM(shape, dtype)

    packs = (rows // 4, GROUP, LANES)
    halos = (rows // 4 + 2, GROUP, LANES)
    out = pl.pallas_call(
        functools.partial(kernel, (n_member, n_domain, n_role, members)),
        name="forecast_analysis",
        out_shape=jax.ShapeDtypeStruct((rows, members, cols), F32),
        in_specs=[
            pl.BlockSpec(memory_space=pltpu.SMEM),
            pl.BlockSpec(memory_space=pl.ANY),
            pl.BlockSpec(memory_space=pltpu.VMEM),
            pl.BlockSpec(memory_space=pltpu.VMEM),
            pl.BlockSpec(memory_space=pltpu.VMEM),
        ],
        out_specs=pl.BlockSpec(memory_space=pl.ANY),
        scratch_shapes=[
            vmem(rows + 8, planes, cols),
            vmem(rows + 8, planes, cols),
            vmem(rows + 8, GROUP, LANES),
            vmem(rows + 8, GROUP, LANES),
            vmem(rows + 8, GROUP, LANES),
            vmem(*packs),
            vmem(*packs),
            vmem(*halos),
            vmem(*halos),
            vmem(rows, members, cols),
            vmem(chunk, total, cols),
            vmem(8, members, LANES),
            vmem(n_role, slot_groups, members, LANES),
            vmem(slot_groups, members, LANES),
            vmem(slot_groups, total, LANES),
            vmem(n_role, gram_rows + GROUP, total),
            vmem(n_role, gram_rows + GROUP, total),
            vmem(gram_rows, total),
            vmem(total, total),
            vmem(total, total),
            vmem(total, total),
            vmem(total, total),
            vmem(total, chunk * cols, dtype=BF16),
            vmem(total, chunk * cols, dtype=BF16),
            vmem(1, chunk * cols),
            vmem(n_member, chunk, members, cols),
            pltpu.SemaphoreType.DMA((3,)),
            pltpu.SemaphoreType.DMA((8,)),
            pltpu.SemaphoreType.DMA((8,)),
            pltpu.SemaphoreType.DMA((6, 8)),
            pltpu.SemaphoreType.DMA((6, 8)),
        ],
        compiler_params=pltpu.CompilerParams(
            collective_id=0, has_side_effects=True, vmem_limit_bytes=40 << 20
        ),
    )(
        count,
        fields,
        cells.reshape(8, LANES),
        values.reshape(8, LANES),
        weights.reshape(8, LANES),
    )
    return jnp.transpose(out, (1, 0, 2))


def solution(mesh):
    sizes = tuple(mesh.shape[a] for a in ("member", "domain", "role"))
    return jax.shard_map(
        functools.partial(shards, sizes),
        mesh=mesh,
        in_specs=(
            P("member", "domain", "role"),
            P("domain", "role"),
            P("domain", "role"),
            P("domain", "role"),
            P("domain", None),
            P("domain"),
            P("domain", None),
            P("domain", None),
        ),
        out_specs=P("member", "domain", "role"),
        check_vma=False,
    )
```

```python
import functools

import jax
import jax.numpy as jnp
from jax import lax
from jax.experimental import pallas as pl
from jax.experimental.pallas import tpu as pltpu
from jax.sharding import PartitionSpec as P

STEPS = 4
ITERS = 6
LANES = 128
GROUP = 8
SEG = 24
F32 = jnp.float32
BF16 = jnp.bfloat16
MESH = pl.DeviceIdType.MESH
NN = (((1,), (0,)), ((), ()))
NT = (((1,), (1,)), ((), ()))


def halves(a):
    high = a.astype(BF16)
    return high, (a - high.astype(F32)).astype(BF16)


def product(a, b, dims=NN):
    (ah, al), (bh, bl) = a, b
    dot = functools.partial(lax.dot_general, dimension_numbers=dims, preferred_element_type=F32)
    return dot(ah, bh) + (dot(ah, bl) + dot(al, bh))


def kernel(
    sizes,
    count_ref,
    ensemble_ref,
    diffusion_hbm,
    drift_rows_hbm,
    drift_cols_hbm,
    cells_hbm,
    values_hbm,
    weights_hbm,
    out_ref,
    raw,
    diffusion_ref,
    drift_rows_ref,
    drift_cols_ref,
    cells_ref,
    values_ref,
    weights_ref,
    top_rows,
    bottom_rows,
    field_a,
    field_b,
    strip_a,
    strip_b,
    strip_coef,
    pack_right,
    pack_left,
    halo_left,
    halo_right,
    final,
    received,
    obs_part,
    obs_role,
    obs_own,
    obs_all,
    gram_part,
    gram_role,
    gram_own,
    gram,
    current,
    inverse,
    mixing,
    dev_high,
    dev_low,
    centre_buf,
    result,
    load_sem,
    small_sem,
    ready_sem,
    halo_send,
    halo_recv,
    peer_send,
    peer_recv,
):
    n_member, n_domain, n_role, members = sizes
    rows = 64
    chunk = rows // n_member
    total = members * n_member
    slot_groups = 8 // n_role
    gram_rows = total // n_role
    groups = members // GROUP
    me_m = lax.axis_index("member")
    me_d = lax.axis_index("domain")
    me_r = lax.axis_index("role")

    def other(me, step, n):
        return lax.rem(me + (step + n), n)

    down, up = other(me_d, 1, n_domain), other(me_d, -1, n_domain)
    right, left = other(me_r, 1, n_role), other(me_r, -1, n_role)
    is_first, is_last = me_d == 0, me_d == n_domain - 1

    load = pltpu.make_async_copy(ensemble_ref, raw, load_sem.at[0])
    load.start()
    smalls = [
        pltpu.make_async_copy(src, dst, small_sem.at[k])
        for k, (src, dst) in enumerate(
            (
                (diffusion_hbm, diffusion_ref),
                (drift_rows_hbm, drift_rows_ref),
                (drift_cols_hbm, drift_cols_ref),
                (cells_hbm, cells_ref),
                (values_hbm, values_ref),
                (weights_hbm, weights_ref),
            )
        )
    ]
    for copy in smalls:
        copy.start()

    barrier = pltpu.get_barrier_semaphore()
    greeted = n_role - 1 + n_member - 1
    columns = (me_r, right, left)

    def greet(sem, domain):
        for r in columns:
            pl.semaphore_signal(sem, inc=1, device_id={"domain": domain, "role": r}, device_id_type=MESH)

    @pl.when(is_first)
    def _():
        greet(barrier, up)

    @pl.when(jnp.logical_not(is_last))
    def _():
        greet(barrier, down)

    for step in range(1, n_role):
        pl.semaphore_signal(barrier, inc=1, device_id={"role": other(me_r, step, n_role)}, device_id_type=MESH)
    for step in range(1, n_member):
        pl.semaphore_signal(barrier, inc=1, device_id={"member": other(me_m, step, n_member)}, device_id_type=MESH)

    lane = lax.broadcasted_iota(jnp.int32, (GROUP, LANES), 1)
    sub = lax.broadcasted_iota(jnp.int32, (GROUP, LANES), 0)
    seg_lane = lane
    for s in range(1, 6):
        seg_lane = jnp.where(lane >= SEG * s, lane - SEG * s, seg_lane)

    for copy in smalls:
        copy.wait()
    load.wait()

    def coef_row(row):
        diffusion = diffusion_ref[pl.ds(row, 1), :]
        drift_rows = drift_rows_ref[pl.ds(row, 1), :]
        drift_cols = drift_cols_ref[pl.ds(row, 1), :]
        keep = 1.0 - 4.0 * diffusion - drift_rows - drift_cols
        behind_row, behind_col = diffusion + drift_rows, diffusion + drift_cols
        return jnp.where(
            sub == 0, keep,
            jnp.where(sub == 1, diffusion, jnp.where(sub == 2, behind_row, behind_col)),
        )

    def turn(i, carry):
        for t in range(8):
            row = 8 * i + t
            field_a[row + 4, :members, :] = raw[pl.ds(row, members, stride=rows), :]
            field_a[row + 4, members:, :] = coef_row(row)
        return carry

    lax.fori_loop(0, rows // 8, turn, 0)
    top_rows[...] = field_a[4:8]
    bottom_rows[...] = field_a[rows : rows + 4]

    def own_strip(row):
        strip = jnp.zeros((GROUP, LANES), F32)
        for s in range(groups + 1):
            block = field_a[row, GROUP * s : GROUP * (s + 1), :]
            base = SEG * s
            ends = pltpu.roll(block, (base + 8) % LANES, 1)
            starts = pltpu.roll(block, (base + 16) % LANES, 1)
            strip = jnp.where((lane >= base) & (lane < base + 8), ends, strip)
            strip = jnp.where((lane >= base + 16) & (lane < base + 24), starts, strip)
        return strip

    def pack(q, carry):
        to_right = to_left = jnp.zeros((GROUP, LANES), F32)
        for t in range(4):
            row = 4 + 4 * q + t
            strip = own_strip(row)
            strip_a[row] = strip
            low, high = 4 + 4 * t, 16 - 4 * t
            moved = pltpu.roll(strip, 4 * t, 1) if t else strip
            to_right = jnp.where((seg_lane >= low) & (seg_lane < low + 4), moved, to_right)
            moved = pltpu.roll(strip, LANES - 4 * t, 1) if t else strip
            to_left = jnp.where((seg_lane >= high) & (seg_lane < high + 4), moved, to_left)
        pack_right[q] = to_right
        pack_left[q] = to_left
        return carry

    after_first = (me_d + n_domain - 1) // n_domain
    at_last = (me_d + 1) // n_domain
    pl.semaphore_wait(barrier, greeted + 3 * after_first + 3 * at_last)

    @pl.when(jnp.logical_not(is_first))
    def _():
        greet(ready_sem.at[0], up)

    @pl.when(is_last)
    def _():
        greet(ready_sem.at[1], down)

    def halo_copy(k, src, dst, where):
        return pltpu.make_async_remote_copy(
            src_ref=src, dst_ref=dst, send_sem=halo_send.at[k], recv_sem=halo_recv.at[k],
            device_id=where, device_id_type=MESH,
        )

    quads = rows // 4
    rows_down = halo_copy(0, bottom_rows, field_a.at[0:4], {"domain": down})
    rows_up = halo_copy(1, top_rows, field_a.at[rows + 4 : rows + 8], {"domain": up})
    sides = [
        halo_copy(2, pack_right, halo_left.at[1 : quads + 1], {"role": right}),
        halo_copy(3, pack_left, halo_right.at[1 : quads + 1], {"role": left}),
    ]
    corners_down = [
        halo_copy(4, pack_right.at[quads - 1], halo_left.at[0], {"domain": down, "role": right}),
        halo_copy(6, pack_left.at[quads - 1], halo_right.at[0], {"domain": down, "role": left}),
    ]
    corners_up = [
        halo_copy(5, pack_right.at[0], halo_left.at[quads + 1], {"domain": up, "role": right}),
        halo_copy(7, pack_left.at[0], halo_right.at[quads + 1], {"domain": up, "role": left}),
    ]

    @pl.when(jnp.logical_not(is_first))
    def _():
        rows_up.start()

    @pl.when(is_last)
    def _():
        rows_down.start()

    lax.fori_loop(0, quads, pack, 0, unroll=2)
    for copy in sides:
        copy.start()

    @pl.when(jnp.logical_not(is_first))
    def _():
        for copy in corners_up:
            copy.start()

    @pl.when(jnp.logical_not(is_last))
    def _():
        pl.semaphore_wait(ready_sem.at[0], 3)
        rows_down.start()

    for copy in corners_down:
        copy.start()

    def advanced(now, before, after, coef):
        axis = now.ndim - 1
        return (
            now * coef[0]
            + (after + pltpu.roll(now, LANES - 1, axis)) * coef[1]
            + before * coef[2]
            + pltpu.roll(now, 1, axis) * coef[3]
        )

    def field_coef(row):
        return [field_a[row, members + k : members + k + 1, :] for k in range(4)]

    def field_rows(source, target, shift, first, amount):
        before = source[first - 1, :members, :]
        now = source[first, :members, :]
        for i in range(amount):
            row = first + i
            after = source[row + 1, :members, :]
            target[row - shift, :members, :] = advanced(now, before, after, field_coef(row))
            before, now = now, after

    def seam_rows(source, first, amount):
        span, back, ahead = (slice(first + k, first + k + amount) for k in (0, -1, 1))
        coef = [strip_coef[span, k : k + 1, :] for k in range(4)]
        return advanced(source[span], source[back], source[ahead], coef)

    def merge(seam, first, amount):
        for i in range(amount):
            for s in range(groups):
                part = slice(GROUP * s, GROUP * (s + 1))
                begin = pltpu.roll(seam[i], (-(SEG * s + 16)) % LANES, 1)
                end = pltpu.roll(seam[i], (120 - SEG * s) % LANES, 1)
                block = final[first - 4 + i, part, :]
                final[first - 4 + i, part, :] = jnp.where(
                    lane < 4, begin, jnp.where(lane >= LANES - 4, end, block)
                )

    fields = (field_a, field_b, field_a, field_b, final)
    strips = (strip_a, strip_b, strip_a, strip_b)
    for step in range(STEPS):
        first, end = 5 + step, rows + 3 - step
        shift = 4 if step == STEPS - 1 else 0
        whole = (end - first) // 10

        def body(i, carry, step=step, first=first, shift=shift):
            field_rows(fields[step], fields[step + 1], shift, first + 10 * i, 10)
            return carry

        lax.fori_loop(0, whole, body, 0)
        if end - first - 10 * whole:
            field_rows(fields[step], fields[step + 1], shift, first + 10 * whole, end - first - 10 * whole)

    for copy in sides:
        copy.wait_recv()

    def unpack(q, carry):
        from_left = halo_left[q]
        from_right = halo_right[q]
        for t in range(4):
            row = 4 * q + t
            strip = strip_a[row]
            moved = pltpu.roll(from_left, (8 - 4 * t) % LANES, 1) if t != 2 else from_left
            strip = jnp.where((seg_lane >= 12) & (seg_lane < 16), moved, strip)
            moved = pltpu.roll(from_right, (4 * t - 8) % LANES, 1) if t != 2 else from_right
            strip = jnp.where((seg_lane >= 8) & (seg_lane < 12), moved, strip)
            strip_a[row] = strip
            coef = strip
            for s in range(groups):
                moved = pltpu.roll(strip, (SEG * (s - groups)) % LANES, 1)
                coef = jnp.where((lane >= SEG * s) & (lane < SEG * (s + 1)), moved, coef)
            strip_coef[row] = coef
        return carry

    lax.fori_loop(1, quads + 1, unpack, 0, unroll=2)

    for step in range(STEPS):
        first, end = 5 + step, rows + 3 - step
        while first < end:
            amount = min(16 if step < STEPS - 1 else 8, end - first)
            seam = seam_rows(strips[step], first, amount)
            if step < STEPS - 1:
                strips[step + 1][first : first + amount] = seam
            else:
                merge(seam, first, amount)
            first += amount

    def edge(first, last):
        for step in range(STEPS):
            shift = 4 if step == STEPS - 1 else 0
            begin = first + step if last else first - step
            field_rows(fields[step], fields[step + 1], shift, begin, 4)
            seam = seam_rows(strips[step], begin, 4)
            if step < STEPS - 1:
                strips[step + 1][begin : begin + 4] = seam
            else:
                merge(seam, begin, 4)

    rows_up.wait_recv()
    for copy in corners_up:
        copy.wait_recv()
    for t in range(4):
        strip_a[rows + 4 + t] = own_strip(rows + 4 + t)
    unpack(quads + 1, 0)
    edge(rows + 3, False)
    def peer_copy(stage, step, src, dst, axis):
        me, n = (me_m, n_member) if axis == "member" else (me_r, n_role)
        return pltpu.make_async_remote_copy(
            src_ref=src, dst_ref=dst, send_sem=peer_send.at[stage, step], recv_sem=peer_recv.at[stage, step],
            device_id={axis: other(me, step, n)}, device_id_type=MESH,
        )

    order = sorted(range(1, n_member), key=lambda s: -min(s, n_member - s))
    mine = pl.ds(pl.multiple_of(members * me_m, members), members)
    forward = {}
    for step in order:
        first = pl.multiple_of(chunk * other(me_m, step, n_member), chunk)
        forward[step] = peer_copy(0, step, final.at[pl.ds(first, chunk)], received.at[:, mine, :], "member")
    keep = pltpu.make_async_copy(
        final.at[pl.ds(pl.multiple_of(chunk * me_m, chunk), chunk)], received.at[:, mine, :], load_sem.at[1]
    )
    early = [s for s in order[::-1] if min(s, n_member - s) <= 2]
    late = [s for s in order if s not in early]

    def start_early(inner):
        for step in early:
            whom = other(me_m, step, n_member)
            ready = whom > 0

            @pl.when(ready if inner else jnp.logical_not(ready))
            def _(copy=forward[step]):
                copy.start()

    start_early(True)

    def observe(begin, part, parts):
        def of_group(g, carry):
            cell = cells_ref[pl.ds(g, 1), :]
            here = ((cell // LANES) % n_role) == me_r
            row_of = jnp.where(here, cell // (LANES * n_role), -1)
            row_of = jnp.broadcast_to(row_of, (members, LANES))
            col_of = jnp.broadcast_to(cell % LANES, (members, LANES))

            def some(q, seen):
                for t in range(part):
                    row = begin + part * q + t
                    picked = jnp.take_along_axis(final[row], col_of, axis=1, mode="promise_in_bounds")
                    seen = jnp.where(row_of == row, picked, seen)
                return seen

            if parts > 1:
                obs_part[g] = lax.fori_loop(0, parts, some, jnp.zeros((members, LANES), F32))
            else:
                obs_part[g] = some(0, obs_part[g])
            return carry

        lax.fori_loop(0, 8, of_group, 0)

    observe(4, 15, 4)

    @pl.when(is_first)
    def _():
        pl.semaphore_wait(ready_sem.at[1], 3)
        rows_up.start()
        for copy in corners_up:
            copy.start()

    rows_down.wait_recv()
    for copy in corners_down:
        copy.wait_recv()
    for t in range(4):
        strip_a[t] = own_strip(t)
    unpack(0, 0)
    edge(1, True)
    start_early(False)
    observe(0, 4, 1)

    def own_groups(r):
        return pl.ds(slot_groups * r, slot_groups)

    copies = []
    for step in range(1, n_role):
        copies.append(
            peer_copy(1, step, obs_part.at[own_groups(other(me_r, step, n_role))], obs_role.at[me_r], "role")
        )
        copies[-1].start()
    obs_role[me_r] = obs_part[own_groups(me_r)]
    for copy in copies:
        copy.wait()
    obs_own[...] = functools.reduce(jnp.add, [obs_role[r] for r in range(n_role)])

    copies = []
    for step in order:
        copies.append(peer_copy(2, step, obs_own, obs_all.at[:, mine, :], "member"))
        copies[-1].start()
    keep.start()
    obs_all[:, mine, :] = obs_own[...]
    for copy in copies:
        copy.wait()
    for step in late:
        forward[step].start()

    part = jnp.zeros((total, total), F32)
    push = jnp.zeros((GROUP, total), F32)
    slot = lax.broadcasted_iota(jnp.int32, (1, LANES), 1)
    for g in range(slot_groups):
        place = slot_groups * me_r + g
        observed = obs_all[g]
        centre = jnp.sum(observed, axis=0, keepdims=True) * (1.0 / total)
        deviation = observed - centre
        usable = slot + place * LANES < count_ref[0]
        weighted = deviation * jnp.where(usable, weights_ref[pl.ds(place, 1), :], 0.0)
        gap = jnp.broadcast_to(values_ref[pl.ds(place, 1), :] - centre, (GROUP, LANES))
        weighted = halves(weighted)
        part = part + product(halves(deviation), weighted, NT)
        push = push + product(halves(gap), weighted, NT)
    for r in range(n_role):
        gram_part[r, :gram_rows, :] = part[gram_rows * r : gram_rows * (r + 1), :]
        gram_part[r, gram_rows:, :] = push

    copies = []
    for step in range(1, n_role):
        copies.append(
            peer_copy(3, step, gram_part.at[other(me_r, step, n_role)], gram_role.at[me_r], "role")
        )
        copies[-1].start()
    gram_role[me_r] = gram_part[me_r]
    for copy in copies:
        copy.wait()
    summed = functools.reduce(jnp.add, [gram_role[r] for r in range(n_role)])
    innovation = summed[gram_rows:, :]
    gram_own[...] = summed[:gram_rows, :]
    band = pl.ds(pl.multiple_of(gram_rows * me_r, gram_rows), gram_rows)
    copies = []
    for step in range(1, n_role):
        copies.append(peer_copy(4, step, gram_own, gram.at[band, :], "role"))
        copies[-1].start()
    gram[band, :] = gram_own[...]
    for copy in copies:
        copy.wait()

    across = lax.broadcasted_iota(jnp.int32, (total, total), 1)
    along = lax.broadcasted_iota(jnp.int32, (total, total), 0)
    diagonal = across == along
    matrix = gram[...] + jnp.where(diagonal, total - 1.0, 0.0)
    squares = jnp.sum(jnp.sum(matrix * matrix, axis=0, keepdims=True), axis=1, keepdims=True)
    scaling = jnp.sqrt(squares)
    scaled = matrix / scaling
    middle = jnp.where(diagonal, 1.5, 0.0) - 0.5 * scaled
    current[...] = product(halves(scaled), halves(middle))
    inverse[...] = middle

    def newton(i, carry):
        cur, inv = halves(current[...]), halves(inverse[...])
        mid = halves(jnp.where(diagonal, 1.5, 0.0) - 0.5 * product(inv, cur))
        current[...] = product(cur, mid)
        inverse[...] = product(mid, inv)
        return carry

    lax.fori_loop(0, ITERS - 2, newton, 0)
    inv = halves(inverse[...])
    mid = halves(jnp.where(diagonal, 1.5, 0.0) - 0.5 * product(inv, halves(current[...])))
    root = product(mid, inv)
    root_halves = halves(root)
    shifted = product(halves(product(halves(innovation), root_halves)), root_halves) / scaling
    mixing[...] = root * jnp.sqrt((total - 1.0) / scaling) + shifted[0:1, :]

    for step in order:
        forward[step].wait()
    keep.wait()
    for i in range(chunk):
        block = received[i]
        centre = jnp.sum(block, axis=0, keepdims=True) * (1.0 / total)
        high, low = halves(block - centre)
        span = slice(LANES * i, LANES * (i + 1))
        dev_high[:, span] = high
        dev_low[:, span] = low
        centre_buf[:, span] = centre

    back = []
    target_rows = pl.ds(pl.multiple_of(chunk * me_m, chunk), chunk)
    for step in order + [0]:
        first = pl.multiple_of(members * other(me_m, step, n_member), members)
        share = halves(mixing[pl.ds(first, members), :])
        updated = product(share, (dev_high[...], dev_low[...])) + centre_buf[...]
        for i in range(chunk):
            result[step, i] = updated[:, LANES * i : LANES * (i + 1)]
        if step:
            copy = peer_copy(5, step, result.at[step], out_ref.at[target_rows], "member")
        else:
            copy = pltpu.make_async_copy(result.at[step], out_ref.at[target_rows], load_sem.at[2])
        copy.start()
        back.append(copy)
    for copy in back[:-1]:
        copy.wait_send()
    for step in order[::-1]:
        back[order.index(step)].wait_recv()
    back[-1].wait()
    for copy in [rows_down, rows_up] + sides + corners_down + corners_up:
        copy.wait_send()


def shards(sizes, ensemble, diffusion, drift_rows, drift_cols, cells, count, values, weights):
    n_member, n_domain, n_role = sizes
    members, rows, cols = ensemble.shape
    total = members * n_member
    planes = members + GROUP
    chunk = rows // n_member
    slot_groups = 8 // n_role
    gram_rows = total // n_role

    def vmem(*shape, dtype=F32):
        return pltpu.VMEM(shape, dtype)

    packs = (rows // 4, GROUP, LANES)
    halos = (rows // 4 + 2, GROUP, LANES)
    out = pl.pallas_call(
        functools.partial(kernel, (n_member, n_domain, n_role, members)),
        name="forecast_analysis",
        out_shape=jax.ShapeDtypeStruct((rows, members, cols), F32),
        in_specs=[pl.BlockSpec(memory_space=pltpu.SMEM)] + [pl.BlockSpec(memory_space=pltpu.HBM)] * 7,
        out_specs=pl.BlockSpec(memory_space=pl.ANY),
        scratch_shapes=[
            vmem(members * rows, cols),
            vmem(rows, cols),
            vmem(rows, cols),
            vmem(rows, cols),
            vmem(8, LANES, dtype=jnp.int32),
            vmem(8, LANES),
            vmem(8, LANES),
            vmem(4, planes, cols),
            vmem(4, planes, cols),
            vmem(rows + 8, planes, cols),
            vmem(rows + 8, planes, cols),
            vmem(rows + 8, GROUP, LANES),
            vmem(rows + 8, GROUP, LANES),
            vmem(rows + 8, GROUP, LANES),
            vmem(*packs),
            vmem(*packs),
            vmem(*halos),
            vmem(*halos),
            vmem(rows, members, cols),
            vmem(chunk, total, cols),
            vmem(8, members, LANES),
            vmem(n_role, slot_groups, members, LANES),
            vmem(slot_groups, members, LANES),
            vmem(slot_groups, total, LANES),
            vmem(n_role, gram_rows + GROUP, total),
            vmem(n_role, gram_rows + GROUP, total),
            vmem(gram_rows, total),
            vmem(total, total),
            vmem(total, total),
            vmem(total, total),
            vmem(total, total),
            vmem(total, chunk * cols, dtype=BF16),
            vmem(total, chunk * cols, dtype=BF16),
            vmem(1, chunk * cols),
            vmem(n_member, chunk, members, cols),
            pltpu.SemaphoreType.DMA((3,)),
            pltpu.SemaphoreType.DMA((6,)),
            pltpu.SemaphoreType.REGULAR((2,)),
            pltpu.SemaphoreType.DMA((8,)),
            pltpu.SemaphoreType.DMA((8,)),
            pltpu.SemaphoreType.DMA((6, 8)),
            pltpu.SemaphoreType.DMA((6, 8)),
        ],
        compiler_params=pltpu.CompilerParams(
            collective_id=0, has_side_effects=True, vmem_limit_bytes=40 << 20
        ),
    )(
        count,
        *(
            pltpu.with_memory_space_constraint(a, pltpu.HBM)
            for a in (
                ensemble.reshape(members * rows, cols),
                diffusion,
                drift_rows,
                drift_cols,
                cells.reshape(8, LANES),
                values.reshape(8, LANES),
                weights.reshape(8, LANES),
            )
        ),
    )
    return jnp.transpose(out, (1, 0, 2))


def solution(mesh):
    sizes = tuple(mesh.shape[a] for a in ("member", "domain", "role"))
    return jax.shard_map(
        functools.partial(shards, sizes),
        mesh=mesh,
        in_specs=(
            P("member", "domain", "role"),
            P("domain", "role"),
            P("domain", "role"),
            P("domain", "role"),
            P("domain", None),
            P("domain"),
            P("domain", None),
            P("domain", None),
        ),
        out_specs=P("member", "domain", "role"),
        check_vma=False,
    )
```

```python
import functools

import jax
import jax.numpy as jnp
from jax import lax
from jax.experimental import pallas as pl
from jax.experimental.pallas import tpu as pltpu
from jax.sharding import PartitionSpec as P

STEPS = 4
ITERS = 6
LANES = 128
GROUP = 8
SEG = 24
F32 = jnp.float32
BF16 = jnp.bfloat16
MESH = pl.DeviceIdType.MESH
NN = (((1,), (0,)), ((), ()))
NT = (((1,), (1,)), ((), ()))


def halves(a):
    high = a.astype(BF16)
    return high, (a - high.astype(F32)).astype(BF16)


def product(a, b, dims=NN):
    (ah, al), (bh, bl) = a, b
    dot = functools.partial(lax.dot_general, dimension_numbers=dims, preferred_element_type=F32)
    return dot(ah, bh) + (dot(ah, bl) + dot(al, bh))


def kernel(
    sizes,
    count_ref,
    ensemble_ref,
    diffusion_hbm,
    drift_rows_hbm,
    drift_cols_hbm,
    cells_hbm,
    values_hbm,
    weights_hbm,
    out_ref,
    raw,
    diffusion_ref,
    drift_rows_ref,
    drift_cols_ref,
    cells_ref,
    values_ref,
    weights_ref,
    top_rows,
    bottom_rows,
    field_a,
    field_b,
    strip_a,
    strip_b,
    strip_coef,
    pack_right,
    pack_left,
    halo_left,
    halo_right,
    final,
    received,
    obs_part,
    obs_role,
    obs_own,
    obs_all,
    gram_part,
    gram_role,
    push_own,
    push_role,
    gram_own,
    gram,
    current,
    inverse,
    mixing,
    dev_high,
    dev_low,
    centre_buf,
    result,
    load_sem,
    small_sem,
    ready_sem,
    halo_send,
    halo_recv,
    peer_send,
    peer_recv,
):
    n_member, n_domain, n_role, members = sizes
    rows = 64
    chunk = rows // n_member
    total = members * n_member
    slot_groups = 8 // n_role
    gram_rows = total // n_role
    groups = members // GROUP
    me_m = lax.axis_index("member")
    me_d = lax.axis_index("domain")
    me_r = lax.axis_index("role")

    def other(me, step, n):
        return lax.rem(me + (step + n), n)

    down, up = other(me_d, 1, n_domain), other(me_d, -1, n_domain)
    right, left = other(me_r, 1, n_role), other(me_r, -1, n_role)
    is_first, is_last = me_d == 0, me_d == n_domain - 1

    load = pltpu.make_async_copy(ensemble_ref, raw, load_sem.at[0])
    load.start()
    smalls = [
        pltpu.make_async_copy(src, dst, small_sem.at[k])
        for k, (src, dst) in enumerate(
            (
                (diffusion_hbm, diffusion_ref),
                (drift_rows_hbm, drift_rows_ref),
                (drift_cols_hbm, drift_cols_ref),
                (cells_hbm, cells_ref),
                (values_hbm, values_ref),
                (weights_hbm, weights_ref),
            )
        )
    ]
    for copy in smalls:
        copy.start()

    barrier = pltpu.get_barrier_semaphore()
    greeted = n_role - 1 + n_member - 1
    columns = (me_r, right, left)

    def greet(sem, domain):
        for r in columns:
            pl.semaphore_signal(sem, inc=1, device_id={"domain": domain, "role": r}, device_id_type=MESH)

    @pl.when(is_first)
    def _():
        greet(barrier, up)

    @pl.when(jnp.logical_not(is_last))
    def _():
        greet(barrier, down)

    for step in range(1, n_role):
        pl.semaphore_signal(barrier, inc=1, device_id={"role": other(me_r, step, n_role)}, device_id_type=MESH)
    for step in range(1, n_member):
        pl.semaphore_signal(barrier, inc=1, device_id={"member": other(me_m, step, n_member)}, device_id_type=MESH)

    lane = lax.broadcasted_iota(jnp.int32, (GROUP, LANES), 1)
    sub = lax.broadcasted_iota(jnp.int32, (GROUP, LANES), 0)
    seg_lane = lane
    for s in range(1, 6):
        seg_lane = jnp.where(lane >= SEG * s, lane - SEG * s, seg_lane)

    for copy in smalls:
        copy.wait()
    load.wait()

    def coef_row(row):
        diffusion = diffusion_ref[pl.ds(row, 1), :]
        drift_rows = drift_rows_ref[pl.ds(row, 1), :]
        drift_cols = drift_cols_ref[pl.ds(row, 1), :]
        keep = 1.0 - 4.0 * diffusion - drift_rows - drift_cols
        behind_row, behind_col = diffusion + drift_rows, diffusion + drift_cols
        return jnp.where(
            sub == 0, keep,
            jnp.where(sub == 1, diffusion, jnp.where(sub == 2, behind_row, behind_col)),
        )

    def turn(i, carry):
        for t in range(8):
            row = 8 * i + t
            field_a[row + 4, :members, :] = raw[pl.ds(row, members, stride=rows), :]
            field_a[row + 4, members:, :] = coef_row(row)
        return carry

    lax.fori_loop(0, rows // 8, turn, 0)
    top_rows[...] = field_a[4:8]
    bottom_rows[...] = field_a[rows : rows + 4]

    def own_strip(row):
        strip = jnp.zeros((GROUP, LANES), F32)
        for s in range(groups + 1):
            block = field_a[row, GROUP * s : GROUP * (s + 1), :]
            base = SEG * s
            ends = pltpu.roll(block, (base + 8) % LANES, 1)
            starts = pltpu.roll(block, (base + 16) % LANES, 1)
            strip = jnp.where((lane >= base) & (lane < base + 8), ends, strip)
            strip = jnp.where((lane >= base + 16) & (lane < base + 24), starts, strip)
        return strip

    def pack(q, carry):
        to_right = to_left = jnp.zeros((GROUP, LANES), F32)
        for t in range(4):
            row = 4 + 4 * q + t
            strip = own_strip(row)
            strip_a[row] = strip
            low, high = 4 + 4 * t, 16 - 4 * t
            moved = pltpu.roll(strip, 4 * t, 1) if t else strip
            to_right = jnp.where((seg_lane >= low) & (seg_lane < low + 4), moved, to_right)
            moved = pltpu.roll(strip, LANES - 4 * t, 1) if t else strip
            to_left = jnp.where((seg_lane >= high) & (seg_lane < high + 4), moved, to_left)
        pack_right[q] = to_right
        pack_left[q] = to_left
        return carry

    after_first = (me_d + n_domain - 1) // n_domain
    at_last = (me_d + 1) // n_domain
    pl.semaphore_wait(barrier, greeted + 3 * after_first + 3 * at_last)

    @pl.when(jnp.logical_not(is_first))
    def _():
        greet(ready_sem.at[0], up)

    @pl.when(is_last)
    def _():
        greet(ready_sem.at[1], down)

    def halo_copy(k, src, dst, where):
        return pltpu.make_async_remote_copy(
            src_ref=src, dst_ref=dst, send_sem=halo_send.at[k], recv_sem=halo_recv.at[k],
            device_id=where, device_id_type=MESH,
        )

    quads = rows // 4
    rows_down = halo_copy(0, bottom_rows, field_a.at[0:4], {"domain": down})
    rows_up = halo_copy(1, top_rows, field_a.at[rows + 4 : rows + 8], {"domain": up})
    sides = [
        halo_copy(2, pack_right, halo_left.at[1 : quads + 1], {"role": right}),
        halo_copy(3, pack_left, halo_right.at[1 : quads + 1], {"role": left}),
    ]
    corners_down = [
        halo_copy(4, pack_right.at[quads - 1], halo_left.at[0], {"domain": down, "role": right}),
        halo_copy(6, pack_left.at[quads - 1], halo_right.at[0], {"domain": down, "role": left}),
    ]
    corners_up = [
        halo_copy(5, pack_right.at[0], halo_left.at[quads + 1], {"domain": up, "role": right}),
        halo_copy(7, pack_left.at[0], halo_right.at[quads + 1], {"domain": up, "role": left}),
    ]

    @pl.when(jnp.logical_not(is_first))
    def _():
        rows_up.start()

    @pl.when(is_last)
    def _():
        rows_down.start()

    pack(quads - 1, 0)
    pack(0, 0)

    @pl.when(is_last)
    def _():
        for copy in corners_down:
            copy.start()

    @pl.when(jnp.logical_not(is_first))
    def _():
        for copy in corners_up:
            copy.start()

    lax.fori_loop(1, quads - 1, pack, 0, unroll=2)
    for copy in sides:
        copy.start()

    def advanced(now, before, after, coef):
        axis = now.ndim - 1
        return (
            now * coef[0]
            + (after + pltpu.roll(now, LANES - 1, axis)) * coef[1]
            + before * coef[2]
            + pltpu.roll(now, 1, axis) * coef[3]
        )

    def field_coef(row):
        return [field_a[row, members + k : members + k + 1, :] for k in range(4)]

    def field_rows(source, target, shift, first, amount):
        before = source[first - 1, :members, :]
        now = source[first, :members, :]
        for i in range(amount):
            row = first + i
            after = source[row + 1, :members, :]
            target[row - shift, :members, :] = advanced(now, before, after, field_coef(row))
            before, now = now, after

    def seam_rows(source, first, amount):
        span, back, ahead = (slice(first + k, first + k + amount) for k in (0, -1, 1))
        coef = [strip_coef[span, k : k + 1, :] for k in range(4)]
        return advanced(source[span], source[back], source[ahead], coef)

    def merge(seam, first, amount):
        for i in range(amount):
            for s in range(groups):
                part = slice(GROUP * s, GROUP * (s + 1))
                begin = pltpu.roll(seam[i], (-(SEG * s + 16)) % LANES, 1)
                end = pltpu.roll(seam[i], (120 - SEG * s) % LANES, 1)
                block = final[first - 4 + i, part, :]
                final[first - 4 + i, part, :] = jnp.where(
                    lane < 4, begin, jnp.where(lane >= LANES - 4, end, block)
                )

    fields = (field_a, field_b, field_a, field_b, final)
    strips = (strip_a, strip_b, strip_a, strip_b)
    for step in range(STEPS):
        first, end = 5 + step, rows + 3 - step
        shift = 4 if step == STEPS - 1 else 0
        half = (end - first) // 2

        def body(i, carry, step=step, first=first, shift=shift, half=half):
            field_rows(fields[step], fields[step + 1], shift, first + half * i, half)
            return carry

        lax.fori_loop(0, 2, body, 0)

    @pl.when(jnp.logical_not(is_last))
    def _():
        pl.semaphore_wait(ready_sem.at[0], 3)
        rows_down.start()
        for copy in corners_down:
            copy.start()

    for copy in sides:
        copy.wait_recv()

    def unpack(q, carry):
        from_left = halo_left[q]
        from_right = halo_right[q]
        for t in range(4):
            row = 4 * q + t
            strip = strip_a[row]
            moved = pltpu.roll(from_left, (8 - 4 * t) % LANES, 1) if t != 2 else from_left
            strip = jnp.where((seg_lane >= 12) & (seg_lane < 16), moved, strip)
            moved = pltpu.roll(from_right, (4 * t - 8) % LANES, 1) if t != 2 else from_right
            strip = jnp.where((seg_lane >= 8) & (seg_lane < 12), moved, strip)
            strip_a[row] = strip
            coef = strip
            for s in range(groups):
                moved = pltpu.roll(strip, (SEG * (s - groups)) % LANES, 1)
                coef = jnp.where((lane >= SEG * s) & (lane < SEG * (s + 1)), moved, coef)
            strip_coef[row] = coef
        return carry

    lax.fori_loop(1, quads + 1, unpack, 0, unroll=4)

    for step in range(STEPS):
        first, end = 5 + step, rows + 3 - step
        while first < end:
            amount = min(31 if step < STEPS - 1 else 14, end - first)
            seam = seam_rows(strips[step], first, amount)
            if step < STEPS - 1:
                strips[step + 1][first : first + amount] = seam
            else:
                merge(seam, first, amount)
            first += amount

    def edge(first, last):
        for step in range(STEPS):
            shift = 4 if step == STEPS - 1 else 0
            begin = first + step if last else first - step
            field_rows(fields[step], fields[step + 1], shift, begin, 4)
            seam = seam_rows(strips[step], begin, 4)
            if step < STEPS - 1:
                strips[step + 1][begin : begin + 4] = seam
            else:
                merge(seam, begin, 4)

    rows_up.wait_recv()
    for copy in corners_up:
        copy.wait_recv()
    for t in range(4):
        strip_a[rows + 4 + t] = own_strip(rows + 4 + t)
    unpack(quads + 1, 0)
    edge(rows + 3, False)
    def peer_copy(stage, step, src, dst, axis):
        me, n = (me_m, n_member) if axis == "member" else (me_r, n_role)
        return pltpu.make_async_remote_copy(
            src_ref=src, dst_ref=dst, send_sem=peer_send.at[stage, step], recv_sem=peer_recv.at[stage, step],
            device_id={axis: other(me, step, n)}, device_id_type=MESH,
        )

    order = sorted(range(1, n_member), key=lambda s: -min(s, n_member - s))
    mine = pl.ds(pl.multiple_of(members * me_m, members), members)
    forward = {}
    for step in order:
        first = pl.multiple_of(chunk * other(me_m, step, n_member), chunk)
        forward[step] = peer_copy(0, step, final.at[pl.ds(first, chunk)], received.at[:, mine, :], "member")
    keep = pltpu.make_async_copy(
        final.at[pl.ds(pl.multiple_of(chunk * me_m, chunk), chunk)], received.at[:, mine, :], load_sem.at[1]
    )
    early = [s for s in order[::-1] if min(s, n_member - s) <= 2]
    late = [s for s in order if s not in early]

    def start_early(inner):
        for step in early:
            whom = other(me_m, step, n_member)
            ready = whom > 0

            @pl.when(ready if inner else jnp.logical_not(ready))
            def _(copy=forward[step]):
                copy.start()

    start_early(True)

    def observe(g, begin, end, seen):
        cell = cells_ref[pl.ds(g, 1), :]
        here = ((cell // LANES) % n_role) == me_r
        row_of = jnp.where(here, cell // (LANES * n_role), -1)
        row_of = jnp.broadcast_to(row_of, (members, LANES))
        col_of = jnp.broadcast_to(cell % LANES, (members, LANES))
        for row in range(begin, end):
            picked = jnp.take_along_axis(final[row], col_of, axis=1, mode="promise_in_bounds")
            seen = jnp.where(row_of == row, picked, seen)
        obs_part[g] = seen

    def observe_group(g, carry):
        observe(g, 4, rows, jnp.zeros((members, LANES), F32))
        return carry

    lax.fori_loop(0, 8, observe_group, 0)

    @pl.when(is_first)
    def _():
        pl.semaphore_wait(ready_sem.at[1], 3)
        rows_up.start()
        for copy in corners_up:
            copy.start()

    rows_down.wait_recv()
    for copy in corners_down:
        copy.wait_recv()
    for t in range(4):
        strip_a[t] = own_strip(t)
    unpack(0, 0)
    edge(1, True)
    start_early(False)

    def own_groups(r):
        return pl.ds(slot_groups * r, slot_groups)

    copies = []
    for step in list(range(1, n_role)) + [0]:
        whom = other(me_r, step, n_role)
        for k in range(slot_groups):
            g = slot_groups * whom + k
            observe(g, 0, 4, obs_part[g])
        if step:
            copies.append(peer_copy(1, step, obs_part.at[own_groups(whom)], obs_role.at[me_r], "role"))
            copies[-1].start()
    obs_role[me_r] = obs_part[own_groups(me_r)]
    for copy in copies:
        copy.wait()
    obs_own[...] = functools.reduce(jnp.add, [obs_role[r] for r in range(n_role)])

    copies = []
    for step in order:
        copies.append(peer_copy(2, step, obs_own, obs_all.at[:, mine, :], "member"))
        copies[-1].start()
    keep.start()
    obs_all[:, mine, :] = obs_own[...]
    for copy in copies:
        copy.wait()
    for step in late:
        forward[step].start()

    part = jnp.zeros((total, total), F32)
    push = jnp.zeros((GROUP, total), F32)
    slot = lax.broadcasted_iota(jnp.int32, (1, LANES), 1)
    for g in range(slot_groups):
        place = slot_groups * me_r + g
        observed = obs_all[g]
        centre = jnp.sum(observed, axis=0, keepdims=True) * (1.0 / total)
        deviation = observed - centre
        usable = slot + place * LANES < count_ref[0]
        weighted = deviation * jnp.where(usable, weights_ref[pl.ds(place, 1), :], 0.0)
        gap = jnp.broadcast_to(values_ref[pl.ds(place, 1), :] - centre, (GROUP, LANES))
        weighted = halves(weighted)
        part = part + product(halves(deviation), weighted, NT)
        push = push + product(halves(gap), weighted, NT)
    for r in range(n_role):
        gram_part[r] = part[gram_rows * r : gram_rows * (r + 1), :]
    push_own[...] = push[0:1, :]

    copies = []
    for step in range(1, n_role):
        copies.append(
            peer_copy(3, step, gram_part.at[other(me_r, step, n_role)], gram_role.at[me_r], "role")
        )
        copies[-1].start()
    pushes = []
    for step in range(1, n_role):
        pushes.append(peer_copy(6, step, push_own, push_role.at[me_r], "role"))
        pushes[-1].start()
    gram_role[me_r] = gram_part[me_r]
    push_role[me_r] = push_own[...]
    for copy in copies:
        copy.wait()
    gram_own[...] = functools.reduce(jnp.add, [gram_role[r] for r in range(n_role)])
    band = pl.ds(pl.multiple_of(gram_rows * me_r, gram_rows), gram_rows)
    copies = []
    for step in range(1, n_role):
        copies.append(peer_copy(4, step, gram_own, gram.at[band, :], "role"))
        copies[-1].start()
    gram[band, :] = gram_own[...]
    for copy in copies:
        copy.wait()

    across = lax.broadcasted_iota(jnp.int32, (total, total), 1)
    along = lax.broadcasted_iota(jnp.int32, (total, total), 0)
    diagonal = across == along
    matrix = gram[...] + jnp.where(diagonal, total - 1.0, 0.0)
    squares = jnp.sum(jnp.sum(matrix * matrix, axis=0, keepdims=True), axis=1, keepdims=True)
    scaling = jnp.sqrt(squares)
    scaled = matrix / scaling
    middle = jnp.where(diagonal, 1.5, 0.0) - 0.5 * scaled
    current[...] = product(halves(scaled), halves(middle))
    inverse[...] = middle

    def newton(i, carry):
        cur, inv = halves(current[...]), halves(inverse[...])
        mid = halves(jnp.where(diagonal, 1.5, 0.0) - 0.5 * product(inv, cur))
        current[...] = product(cur, mid)
        inverse[...] = product(mid, inv)
        return carry

    lax.fori_loop(0, ITERS - 2, newton, 0)
    for copy in pushes:
        copy.wait()
    innovation = functools.reduce(jnp.add, [push_role[r] for r in range(n_role)])
    innovation = jnp.broadcast_to(innovation, (GROUP, total))
    inv = halves(inverse[...])
    mid = halves(jnp.where(diagonal, 1.5, 0.0) - 0.5 * product(inv, halves(current[...])))
    root = product(mid, inv)
    root_halves = halves(root)
    shifted = product(halves(product(halves(innovation), root_halves)), root_halves) / scaling
    mixing[...] = root * jnp.sqrt((total - 1.0) / scaling) + shifted[0:1, :]

    for step in order:
        forward[step].wait()
    keep.wait()
    for i in range(chunk):
        block = received[i]
        centre = jnp.sum(block, axis=0, keepdims=True) * (1.0 / total)
        high, low = halves(block - centre)
        span = slice(LANES * i, LANES * (i + 1))
        dev_high[:, span] = high
        dev_low[:, span] = low
        centre_buf[:, span] = centre

    back = []
    target_rows = pl.ds(pl.multiple_of(chunk * me_m, chunk), chunk)
    for step in order + [0]:
        first = pl.multiple_of(members * other(me_m, step, n_member), members)
        share = halves(mixing[pl.ds(first, members), :])
        updated = product(share, (dev_high[...], dev_low[...])) + centre_buf[...]
        for i in range(chunk):
            result[step, i] = updated[:, LANES * i : LANES * (i + 1)]
        if step:
            copy = peer_copy(5, step, result.at[step], out_ref.at[target_rows], "member")
        else:
            copy = pltpu.make_async_copy(result.at[step], out_ref.at[target_rows], load_sem.at[2])
        copy.start()
        back.append(copy)
    for copy in back[:-1]:
        copy.wait_send()
    for step in order[::-1]:
        back[order.index(step)].wait_recv()
    back[-1].wait()
    for copy in [rows_down, rows_up] + sides + corners_down + corners_up:
        copy.wait_send()


def shards(sizes, ensemble, diffusion, drift_rows, drift_cols, cells, count, values, weights):
    n_member, n_domain, n_role = sizes
    members, rows, cols = ensemble.shape
    total = members * n_member
    planes = members + GROUP
    chunk = rows // n_member
    slot_groups = 8 // n_role
    gram_rows = total // n_role

    def vmem(*shape, dtype=F32):
        return pltpu.VMEM(shape, dtype)

    packs = (rows // 4, GROUP, LANES)
    halos = (rows // 4 + 2, GROUP, LANES)
    out = pl.pallas_call(
        functools.partial(kernel, (n_member, n_domain, n_role, members)),
        name="forecast_analysis",
        out_shape=jax.ShapeDtypeStruct((rows, members, cols), F32),
        in_specs=[pl.BlockSpec(memory_space=pltpu.SMEM)] + [pl.BlockSpec(memory_space=pltpu.HBM)] * 7,
        out_specs=pl.BlockSpec(memory_space=pl.ANY),
        scratch_shapes=[
            vmem(members * rows, cols),
            vmem(rows, cols),
            vmem(rows, cols),
            vmem(rows, cols),
            vmem(8, LANES, dtype=jnp.int32),
            vmem(8, LANES),
            vmem(8, LANES),
            vmem(4, planes, cols),
            vmem(4, planes, cols),
            vmem(rows + 8, planes, cols),
            vmem(rows + 8, planes, cols),
            vmem(rows + 8, GROUP, LANES),
            vmem(rows + 8, GROUP, LANES),
            vmem(rows + 8, GROUP, LANES),
            vmem(*packs),
            vmem(*packs),
            vmem(*halos),
            vmem(*halos),
            vmem(rows, members, cols),
            vmem(chunk, total, cols),
            vmem(8, members, LANES),
            vmem(n_role, slot_groups, members, LANES),
            vmem(slot_groups, members, LANES),
            vmem(slot_groups, total, LANES),
            vmem(n_role, gram_rows, total),
            vmem(n_role, gram_rows, total),
            vmem(1, total),
            vmem(n_role, 1, total),
            vmem(gram_rows, total),
            vmem(total, total),
            vmem(total, total),
            vmem(total, total),
            vmem(total, total),
            vmem(total, chunk * cols, dtype=BF16),
            vmem(total, chunk * cols, dtype=BF16),
            vmem(1, chunk * cols),
            vmem(n_member, chunk, members, cols),
            pltpu.SemaphoreType.DMA((3,)),
            pltpu.SemaphoreType.DMA((6,)),
            pltpu.SemaphoreType.REGULAR((2,)),
            pltpu.SemaphoreType.DMA((8,)),
            pltpu.SemaphoreType.DMA((8,)),
            pltpu.SemaphoreType.DMA((7, 8)),
            pltpu.SemaphoreType.DMA((7, 8)),
        ],
        compiler_params=pltpu.CompilerParams(
            collective_id=0, has_side_effects=True, vmem_limit_bytes=40 << 20
        ),
    )(
        count,
        *(
            pltpu.with_memory_space_constraint(a, pltpu.HBM)
            for a in (
                ensemble.reshape(members * rows, cols),
                diffusion,
                drift_rows,
                drift_cols,
                cells.reshape(8, LANES),
                values.reshape(8, LANES),
                weights.reshape(8, LANES),
            )
        ),
    )
    return jnp.transpose(out, (1, 0, 2))


def solution(mesh):
    sizes = tuple(mesh.shape[a] for a in ("member", "domain", "role"))
    return jax.shard_map(
        functools.partial(shards, sizes),
        mesh=mesh,
        in_specs=(
            P("member", "domain", "role"),
            P("domain", "role"),
            P("domain", "role"),
            P("domain", "role"),
            P("domain", None),
            P("domain"),
            P("domain", None),
            P("domain", None),
        ),
        out_specs=P("member", "domain", "role"),
        check_vma=False,
    )
```

```python
import functools

import jax
import jax.numpy as jnp
from jax import lax
from jax.experimental import pallas as pl
from jax.experimental.pallas import tpu as pltpu
from jax.sharding import PartitionSpec as P

STEPS = 4
ITERS = 6
LANES = 128
GROUP = 8
SEG = 24
F32 = jnp.float32
BF16 = jnp.bfloat16
MESH = pl.DeviceIdType.MESH
NN = (((1,), (0,)), ((), ()))
NT = (((1,), (1,)), ((), ()))


def halves(a):
    high = a.astype(BF16)
    return high, (a - high.astype(F32)).astype(BF16)


def product(a, b, dims=NN):
    (ah, al), (bh, bl) = a, b
    dot = functools.partial(lax.dot_general, dimension_numbers=dims, preferred_element_type=F32)
    return dot(ah, bh) + (dot(ah, bl) + dot(al, bh))


def kernel(
    sizes,
    count_ref,
    ensemble_ref,
    diffusion_hbm,
    drift_rows_hbm,
    drift_cols_hbm,
    cells_hbm,
    values_hbm,
    weights_hbm,
    out_ref,
    raw,
    diffusion_ref,
    drift_rows_ref,
    drift_cols_ref,
    cells_ref,
    values_ref,
    weights_ref,
    top_rows,
    bottom_rows,
    field_a,
    field_b,
    strip_a,
    strip_b,
    strip_coef,
    pack_right,
    pack_left,
    halo_left,
    halo_right,
    final,
    received,
    obs_part,
    obs_role,
    obs_own,
    obs_all,
    gram_part,
    gram_role,
    push_own,
    push_role,
    gram_own,
    gram,
    current,
    inverse,
    mixing,
    dev_high,
    dev_low,
    centre_buf,
    result,
    load_sem,
    whole_sem,
    small_sem,
    ready_sem,
    halo_send,
    halo_recv,
    peer_send,
    peer_recv,
):
    n_member, n_domain, n_role, members = sizes
    rows = 64
    chunk = rows // n_member
    total = members * n_member
    slot_groups = 8 // n_role
    gram_rows = total // n_role
    groups = members // GROUP
    me_m = lax.axis_index("member")
    me_d = lax.axis_index("domain")
    me_r = lax.axis_index("role")

    def other(me, step, n):
        return lax.rem(me + (step + n), n)

    down, up = other(me_d, 1, n_domain), other(me_d, -1, n_domain)
    right, left = other(me_r, 1, n_role), other(me_r, -1, n_role)
    is_first, is_last = me_d == 0, me_d == n_domain - 1

    quarter = members * rows // 4
    loads = [
        pltpu.make_async_copy(
            ensemble_ref.at[k * quarter : (k + 1) * quarter], raw.at[k * quarter : (k + 1) * quarter], whole_sem.at[k]
        )
        for k in range(4)
    ]
    for copy in loads:
        copy.start()
    smalls = [
        pltpu.make_async_copy(src, dst, small_sem.at[k])
        for k, (src, dst) in enumerate(
            (
                (diffusion_hbm, diffusion_ref),
                (drift_rows_hbm, drift_rows_ref),
                (drift_cols_hbm, drift_cols_ref),
                (cells_hbm, cells_ref),
                (values_hbm, values_ref),
                (weights_hbm, weights_ref),
            )
        )
    ]
    for copy in smalls:
        copy.start()

    barrier = pltpu.get_barrier_semaphore()
    greeted = n_role - 1 + n_member - 1
    columns = (me_r, right, left)

    def greet(sem, domain):
        for r in columns:
            pl.semaphore_signal(sem, inc=1, device_id={"domain": domain, "role": r}, device_id_type=MESH)

    @pl.when(is_first)
    def _():
        greet(barrier, up)

    @pl.when(jnp.logical_not(is_last))
    def _():
        greet(barrier, down)

    for step in range(1, n_role):
        pl.semaphore_signal(barrier, inc=1, device_id={"role": other(me_r, step, n_role)}, device_id_type=MESH)
    for step in range(1, n_member):
        pl.semaphore_signal(barrier, inc=1, device_id={"member": other(me_m, step, n_member)}, device_id_type=MESH)

    lane = lax.broadcasted_iota(jnp.int32, (GROUP, LANES), 1)
    sub = lax.broadcasted_iota(jnp.int32, (GROUP, LANES), 0)
    seg_lane = lane
    for s in range(1, 6):
        seg_lane = jnp.where(lane >= SEG * s, lane - SEG * s, seg_lane)

    for copy in smalls + loads:
        copy.wait()

    def coef_row(row):
        diffusion = diffusion_ref[pl.ds(row, 1), :]
        drift_rows = drift_rows_ref[pl.ds(row, 1), :]
        drift_cols = drift_cols_ref[pl.ds(row, 1), :]
        keep = 1.0 - 4.0 * diffusion - drift_rows - drift_cols
        behind_row, behind_col = diffusion + drift_rows, diffusion + drift_cols
        return jnp.where(
            sub == 0, keep,
            jnp.where(sub == 1, diffusion, jnp.where(sub == 2, behind_row, behind_col)),
        )

    def turn(i, carry):
        for t in range(8):
            row = 8 * i + t
            field_a[row + 4, :members, :] = raw[pl.ds(row, members, stride=rows), :]
            field_a[row + 4, members:, :] = coef_row(row)
        return carry

    lax.fori_loop(0, rows // 8, turn, 0)
    top_rows[...] = field_a[4:8]
    bottom_rows[...] = field_a[rows : rows + 4]

    def stacked(pieces, masks):
        whole = pieces[0]
        for piece, mask in zip(pieces[1:], masks):
            whole = jnp.where(mask, piece, whole)
        return whole

    def turned(value, shift):
        return pltpu.roll(value, shift % LANES, value.ndim - 1) if shift % LANES else value

    strip_masks = [lane >= SEG * (k // 2) + 16 * (k % 2) for k in range(1, 2 * groups + 2)]
    quad_masks = [seg_lane >= 8, seg_lane >= 12, seg_lane >= 16]
    halo_mask = quad_masks[0] & (seg_lane < 16)
    seg_masks = [lane >= SEG * s for s in range(1, groups)]

    def own_strip(row):
        pieces = []
        for s in range(groups + 1):
            block = field_a[row, GROUP * s : GROUP * (s + 1), :]
            pieces += [turned(block, SEG * s + 8), turned(block, SEG * s + 16)]
        return stacked(pieces, strip_masks)

    def pack(q):
        own = [strip_a[4 + 4 * q + t] for t in range(4)]
        pack_right[q] = stacked([turned(own[t], 4 * t) for t in range(4)], quad_masks)
        pack_left[q] = stacked([turned(own[t], -4 * t) for t in range(3, -1, -1)], quad_masks)

    def own_strips(first, amount):
        for t in range(amount):
            strip_a[first + t] = own_strip(first + t)

    def own_block(i, carry):
        own_strips(8 + 14 * i, 14)
        return carry

    after_first = (me_d + n_domain - 1) // n_domain
    at_last = (me_d + 1) // n_domain
    pl.semaphore_wait(barrier, greeted + 3 * after_first + 3 * at_last)

    @pl.when(jnp.logical_not(is_first))
    def _():
        greet(ready_sem.at[0], up)

    @pl.when(is_last)
    def _():
        greet(ready_sem.at[1], down)

    def halo_copy(k, src, dst, where):
        return pltpu.make_async_remote_copy(
            src_ref=src, dst_ref=dst, send_sem=halo_send.at[k], recv_sem=halo_recv.at[k],
            device_id=where, device_id_type=MESH,
        )

    quads = rows // 4
    rows_down = halo_copy(0, bottom_rows, field_a.at[0:4], {"domain": down})
    rows_up = halo_copy(1, top_rows, field_a.at[rows + 4 : rows + 8], {"domain": up})
    sides = [
        halo_copy(2, pack_right, halo_left.at[1 : quads + 1], {"role": right}),
        halo_copy(3, pack_left, halo_right.at[1 : quads + 1], {"role": left}),
    ]
    corners_down = [
        halo_copy(4, pack_right.at[quads - 1], halo_left.at[0], {"domain": down, "role": right}),
        halo_copy(6, pack_left.at[quads - 1], halo_right.at[0], {"domain": down, "role": left}),
    ]
    corners_up = [
        halo_copy(5, pack_right.at[0], halo_left.at[quads + 1], {"domain": up, "role": right}),
        halo_copy(7, pack_left.at[0], halo_right.at[quads + 1], {"domain": up, "role": left}),
    ]

    @pl.when(jnp.logical_not(is_first))
    def _():
        rows_up.start()

    @pl.when(is_last)
    def _():
        rows_down.start()

    own_strips(4, 4)
    own_strips(rows, 4)
    pack(quads - 1)
    pack(0)

    @pl.when(is_last)
    def _():
        for copy in corners_down:
            copy.start()

    @pl.when(jnp.logical_not(is_first))
    def _():
        for copy in corners_up:
            copy.start()

    lax.fori_loop(0, 4, own_block, 0)
    for q in range(1, quads - 1):
        pack(q)
    for copy in sides:
        copy.start()

    def advanced(now, before, after, coef):
        axis = now.ndim - 1
        return (
            now * coef[0]
            + (after + pltpu.roll(now, LANES - 1, axis)) * coef[1]
            + before * coef[2]
            + pltpu.roll(now, 1, axis) * coef[3]
        )

    def field_coef(row):
        return [field_a[row, members + k : members + k + 1, :] for k in range(4)]

    def field_rows(source, target, shift, first, amount):
        before = source[first - 1, :members, :]
        now = source[first, :members, :]
        for i in range(amount):
            row = first + i
            after = source[row + 1, :members, :]
            target[row - shift, :members, :] = advanced(now, before, after, field_coef(row))
            before, now = now, after

    def seam_rows(source, first, amount):
        span, back, ahead = (slice(first + k, first + k + amount) for k in (0, -1, 1))
        coef = [strip_coef[span, k : k + 1, :] for k in range(4)]
        return advanced(source[span], source[back], source[ahead], coef)

    def merge(seam, first, amount):
        for i in range(amount):
            for s in range(groups):
                part = slice(GROUP * s, GROUP * (s + 1))
                begin = pltpu.roll(seam[i], (-(SEG * s + 16)) % LANES, 1)
                end = pltpu.roll(seam[i], (120 - SEG * s) % LANES, 1)
                block = final[first - 4 + i, part, :]
                final[first - 4 + i, part, :] = jnp.where(
                    lane < 4, begin, jnp.where(lane >= LANES - 4, end, block)
                )

    fields = (field_a, field_b, field_a, field_b, final)
    strips = (strip_a, strip_b, strip_a, strip_b)
    for step in range(STEPS):
        first, end = 5 + step, rows + 3 - step
        shift = 4 if step == STEPS - 1 else 0
        field_rows(fields[step], fields[step + 1], shift, first, end - first)

    @pl.when(jnp.logical_not(is_last))
    def _():
        pl.semaphore_wait(ready_sem.at[0], 3)
        rows_down.start()
        for copy in corners_down:
            copy.start()

    for copy in sides:
        copy.wait_recv()

    def unpack(q, carry):
        from_left = halo_left[q]
        from_right = halo_right[q]
        for t in range(4):
            row = 4 * q + t
            halo = jnp.where(quad_masks[1], turned(from_left, 8 - 4 * t), turned(from_right, 4 * t - 8))
            strip = jnp.where(halo_mask, halo, strip_a[row])
            strip_a[row] = strip
            strip_coef[row] = stacked([turned(strip, SEG * (s - groups)) for s in range(groups)], seg_masks)
        return carry

    lax.fori_loop(1, quads + 1, unpack, 0, unroll=4)

    for step in range(STEPS):
        first, end = 5 + step, rows + 3 - step
        while first < end:
            amount = min(31 if step < STEPS - 1 else 14, end - first)
            seam = seam_rows(strips[step], first, amount)
            if step < STEPS - 1:
                strips[step + 1][first : first + amount] = seam
            else:
                merge(seam, first, amount)
            first += amount

    def edge(first, last):
        for step in range(STEPS):
            shift = 4 if step == STEPS - 1 else 0
            begin = first + step if last else first - step
            field_rows(fields[step], fields[step + 1], shift, begin, 4)
            seam = seam_rows(strips[step], begin, 4)
            if step < STEPS - 1:
                strips[step + 1][begin : begin + 4] = seam
            else:
                merge(seam, begin, 4)

    rows_up.wait_recv()
    for copy in corners_up:
        copy.wait_recv()
    for t in range(4):
        strip_a[rows + 4 + t] = own_strip(rows + 4 + t)
    unpack(quads + 1, 0)
    edge(rows + 3, False)
    def peer_copy(stage, step, src, dst, axis):
        me, n = (me_m, n_member) if axis == "member" else (me_r, n_role)
        return pltpu.make_async_remote_copy(
            src_ref=src, dst_ref=dst, send_sem=peer_send.at[stage, step], recv_sem=peer_recv.at[stage, step],
            device_id={axis: other(me, step, n)}, device_id_type=MESH,
        )

    order = sorted(range(1, n_member), key=lambda s: -min(s, n_member - s))
    mine = pl.ds(pl.multiple_of(members * me_m, members), members)
    forward = {}
    for step in order:
        first = pl.multiple_of(chunk * other(me_m, step, n_member), chunk)
        forward[step] = peer_copy(0, step, final.at[pl.ds(first, chunk)], received.at[:, mine, :], "member")
    keep = pltpu.make_async_copy(
        final.at[pl.ds(pl.multiple_of(chunk * me_m, chunk), chunk)], received.at[:, mine, :], load_sem.at[1]
    )
    early = [s for s in order[::-1] if min(s, n_member - s) <= 2]
    late = [s for s in order if s not in early]

    def start_early(inner):
        for step in early:
            whom = other(me_m, step, n_member)
            ready = whom > 0

            @pl.when(ready if inner else jnp.logical_not(ready))
            def _(copy=forward[step]):
                copy.start()

    start_early(True)

    def observe(g, begin, end, seen):
        cell = cells_ref[pl.ds(g, 1), :]
        here = ((cell // LANES) % n_role) == me_r
        row_of = jnp.where(here, cell // (LANES * n_role), -1)
        row_of = jnp.broadcast_to(row_of, (members, LANES))
        col_of = jnp.broadcast_to(cell % LANES, (members, LANES))
        for row in range(begin, end):
            picked = jnp.take_along_axis(final[row], col_of, axis=1, mode="promise_in_bounds")
            seen = jnp.where(row_of == row, picked, seen)
        obs_part[g] = seen

    def observe_group(g, carry):
        for k in range(2):
            observe(2 * g + k, 4, rows, jnp.zeros((members, LANES), F32))
        return carry

    lax.fori_loop(0, 4, observe_group, 0)

    @pl.when(is_first)
    def _():
        pl.semaphore_wait(ready_sem.at[1], 3)
        rows_up.start()
        for copy in corners_up:
            copy.start()

    rows_down.wait_recv()
    for copy in corners_down:
        copy.wait_recv()
    for t in range(4):
        strip_a[t] = own_strip(t)
    unpack(0, 0)
    edge(1, True)
    start_early(False)

    def own_groups(r):
        return pl.ds(slot_groups * r, slot_groups)

    copies = []
    for step in list(range(1, n_role)) + [0]:
        whom = other(me_r, step, n_role)
        for k in range(slot_groups):
            g = slot_groups * whom + k
            observe(g, 0, 4, obs_part[g])
        if step:
            copies.append(peer_copy(1, step, obs_part.at[own_groups(whom)], obs_role.at[me_r], "role"))
            copies[-1].start()
    obs_role[me_r] = obs_part[own_groups(me_r)]
    for copy in copies:
        copy.wait()
    obs_own[...] = functools.reduce(jnp.add, [obs_role[r] for r in range(n_role)])

    copies = []
    for step in order:
        copies.append(peer_copy(2, step, obs_own, obs_all.at[:, mine, :], "member"))
        copies[-1].start()
    keep.start()
    obs_all[:, mine, :] = obs_own[...]
    for copy in copies:
        copy.wait()
    for step in late:
        forward[step].start()

    part = jnp.zeros((total, total), F32)
    push = jnp.zeros((GROUP, total), F32)
    slot = lax.broadcasted_iota(jnp.int32, (1, LANES), 1)
    for g in range(slot_groups):
        place = slot_groups * me_r + g
        observed = obs_all[g]
        centre = jnp.sum(observed, axis=0, keepdims=True) * (1.0 / total)
        deviation = observed - centre
        usable = slot + place * LANES < count_ref[0]
        weighted = deviation * jnp.where(usable, weights_ref[pl.ds(place, 1), :], 0.0)
        gap = jnp.broadcast_to(values_ref[pl.ds(place, 1), :] - centre, (GROUP, LANES))
        weighted = halves(weighted)
        part = part + product(halves(deviation), weighted, NT)
        push = push + product(halves(gap), weighted, NT)
    for r in range(n_role):
        gram_part[r] = part[gram_rows * r : gram_rows * (r + 1), :]
    push_own[...] = push[0:1, :]

    copies = []
    for step in range(1, n_role):
        copies.append(
            peer_copy(3, step, gram_part.at[other(me_r, step, n_role)], gram_role.at[me_r], "role")
        )
        copies[-1].start()
    pushes = []
    for step in range(1, n_role):
        pushes.append(peer_copy(6, step, push_own, push_role.at[me_r], "role"))
        pushes[-1].start()
    gram_role[me_r] = gram_part[me_r]
    push_role[me_r] = push_own[...]
    for copy in copies:
        copy.wait()
    gram_own[...] = functools.reduce(jnp.add, [gram_role[r] for r in range(n_role)])
    band = pl.ds(pl.multiple_of(gram_rows * me_r, gram_rows), gram_rows)
    copies = []
    for step in range(1, n_role):
        copies.append(peer_copy(4, step, gram_own, gram.at[band, :], "role"))
        copies[-1].start()
    gram[band, :] = gram_own[...]
    for copy in copies:
        copy.wait()

    across = lax.broadcasted_iota(jnp.int32, (total, total), 1)
    along = lax.broadcasted_iota(jnp.int32, (total, total), 0)
    diagonal = across == along
    matrix = gram[...] + jnp.where(diagonal, total - 1.0, 0.0)
    squares = jnp.sum(jnp.sum(matrix * matrix, axis=0, keepdims=True), axis=1, keepdims=True)
    scaling = jnp.sqrt(squares)
    scaled = matrix / scaling
    middle = jnp.where(diagonal, 1.5, 0.0) - 0.5 * scaled
    current[...] = product(halves(scaled), halves(middle))
    inverse[...] = middle

    def newton(i, carry):
        cur, inv = halves(current[...]), halves(inverse[...])
        mid = halves(jnp.where(diagonal, 1.5, 0.0) - 0.5 * product(inv, cur))
        current[...] = product(cur, mid)
        inverse[...] = product(mid, inv)
        return carry

    lax.fori_loop(0, ITERS - 2, newton, 0)
    for copy in pushes:
        copy.wait()
    innovation = functools.reduce(jnp.add, [push_role[r] for r in range(n_role)])
    innovation = jnp.broadcast_to(innovation, (GROUP, total))
    inv = halves(inverse[...])
    mid = halves(jnp.where(diagonal, 1.5, 0.0) - 0.5 * product(inv, halves(current[...])))
    root = product(mid, inv)
    root_halves = halves(root)
    shifted = product(halves(product(halves(innovation), root_halves)), root_halves) / scaling
    mixing[...] = root * jnp.sqrt((total - 1.0) / scaling) + shifted[0:1, :]

    for step in order:
        forward[step].wait()
    keep.wait()
    for i in range(chunk):
        block = received[i]
        centre = jnp.sum(block, axis=0, keepdims=True) * (1.0 / total)
        high, low = halves(block - centre)
        span = slice(LANES * i, LANES * (i + 1))
        dev_high[:, span] = high
        dev_low[:, span] = low
        centre_buf[:, span] = centre

    back = []
    target_rows = pl.ds(pl.multiple_of(chunk * me_m, chunk), chunk)
    for step in order + [0]:
        first = pl.multiple_of(members * other(me_m, step, n_member), members)
        share = halves(mixing[pl.ds(first, members), :])
        updated = product(share, (dev_high[...], dev_low[...])) + centre_buf[...]
        for i in range(chunk):
            result[step, i] = updated[:, LANES * i : LANES * (i + 1)]
        if step:
            copy = peer_copy(5, step, result.at[step], out_ref.at[target_rows], "member")
        else:
            copy = pltpu.make_async_copy(result.at[step], out_ref.at[target_rows], load_sem.at[2])
        copy.start()
        back.append(copy)
    for copy in back[:-1]:
        copy.wait_send()
    for step in order[::-1]:
        back[order.index(step)].wait_recv()
    back[-1].wait()
    for copy in [rows_down, rows_up] + sides + corners_down + corners_up:
        copy.wait_send()


def shards(sizes, ensemble, diffusion, drift_rows, drift_cols, cells, count, values, weights):
    n_member, n_domain, n_role = sizes
    members, rows, cols = ensemble.shape
    total = members * n_member
    planes = members + GROUP
    chunk = rows // n_member
    slot_groups = 8 // n_role
    gram_rows = total // n_role

    def vmem(*shape, dtype=F32):
        return pltpu.VMEM(shape, dtype)

    packs = (rows // 4, GROUP, LANES)
    halos = (rows // 4 + 2, GROUP, LANES)
    out = pl.pallas_call(
        functools.partial(kernel, (n_member, n_domain, n_role, members)),
        name="forecast_analysis",
        out_shape=jax.ShapeDtypeStruct((rows, members, cols), F32),
        in_specs=[pl.BlockSpec(memory_space=pltpu.SMEM)] + [pl.BlockSpec(memory_space=pltpu.HBM)] * 7,
        out_specs=pl.BlockSpec(memory_space=pl.ANY),
        scratch_shapes=[
            vmem(members * rows, cols),
            vmem(rows, cols),
            vmem(rows, cols),
            vmem(rows, cols),
            vmem(8, LANES, dtype=jnp.int32),
            vmem(8, LANES),
            vmem(8, LANES),
            vmem(4, planes, cols),
            vmem(4, planes, cols),
            vmem(rows + 8, planes, cols),
            vmem(rows + 8, planes, cols),
            vmem(rows + 8, GROUP, LANES),
            vmem(rows + 8, GROUP, LANES),
            vmem(rows + 8, GROUP, LANES),
            vmem(*packs),
            vmem(*packs),
            vmem(*halos),
            vmem(*halos),
            vmem(rows, members, cols),
            vmem(chunk, total, cols),
            vmem(8, members, LANES),
            vmem(n_role, slot_groups, members, LANES),
            vmem(slot_groups, members, LANES),
            vmem(slot_groups, total, LANES),
            vmem(n_role, gram_rows, total),
            vmem(n_role, gram_rows, total),
            vmem(1, total),
            vmem(n_role, 1, total),
            vmem(gram_rows, total),
            vmem(total, total),
            vmem(total, total),
            vmem(total, total),
            vmem(total, total),
            vmem(total, chunk * cols, dtype=BF16),
            vmem(total, chunk * cols, dtype=BF16),
            vmem(1, chunk * cols),
            vmem(n_member, chunk, members, cols),
            pltpu.SemaphoreType.DMA((3,)),
            pltpu.SemaphoreType.DMA((4,)),
            pltpu.SemaphoreType.DMA((6,)),
            pltpu.SemaphoreType.REGULAR((2,)),
            pltpu.SemaphoreType.DMA((8,)),
            pltpu.SemaphoreType.DMA((8,)),
            pltpu.SemaphoreType.DMA((7, 8)),
            pltpu.SemaphoreType.DMA((7, 8)),
        ],
        compiler_params=pltpu.CompilerParams(
            collective_id=0, has_side_effects=True, vmem_limit_bytes=40 << 20
        ),
    )(
        count,
        *(
            pltpu.with_memory_space_constraint(a, pltpu.HBM)
            for a in (
                ensemble.reshape(members * rows, cols),
                diffusion,
                drift_rows,
                drift_cols,
                cells.reshape(8, LANES),
                values.reshape(8, LANES),
                weights.reshape(8, LANES),
            )
        ),
    )
    return jnp.transpose(out, (1, 0, 2))


def solution(mesh):
    sizes = tuple(mesh.shape[a] for a in ("member", "domain", "role"))
    return jax.shard_map(
        functools.partial(shards, sizes),
        mesh=mesh,
        in_specs=(
            P("member", "domain", "role"),
            P("domain", "role"),
            P("domain", "role"),
            P("domain", "role"),
            P("domain", None),
            P("domain"),
            P("domain", None),
            P("domain", None),
        ),
        out_specs=P("member", "domain", "role"),
        check_vma=False,
    )
```

```python
import functools

import jax
import jax.numpy as jnp
from jax import lax
from jax.experimental import pallas as pl
from jax.experimental.pallas import tpu as pltpu
from jax.sharding import PartitionSpec as P

STEPS = 4
ITERS = 6
LANES = 128
GROUP = 8
SEG = 24
F32 = jnp.float32
BF16 = jnp.bfloat16
MESH = pl.DeviceIdType.MESH
NN = (((1,), (0,)), ((), ()))
NT = (((1,), (1,)), ((), ()))


def halves(a):
    high = a.astype(BF16)
    return high, (a - high.astype(F32)).astype(BF16)


def product(a, b, dims=NN):
    (ah, al), (bh, bl) = a, b
    dot = functools.partial(lax.dot_general, dimension_numbers=dims, preferred_element_type=F32)
    return dot(ah, bh) + (dot(ah, bl) + dot(al, bh))


def kernel(
    sizes,
    count_ref,
    ensemble_ref,
    diffusion_hbm,
    drift_rows_hbm,
    drift_cols_hbm,
    cells_hbm,
    values_hbm,
    weights_hbm,
    out_ref,
    raw,
    diffusion_ref,
    drift_rows_ref,
    drift_cols_ref,
    cells_ref,
    values_ref,
    weights_ref,
    top_rows,
    bottom_rows,
    field_a,
    field_b,
    strip_a,
    strip_b,
    strip_coef,
    pack_right,
    pack_left,
    halo_left,
    halo_right,
    final,
    received,
    obs_part,
    obs_role,
    obs_own,
    obs_all,
    gram_part,
    gram_role,
    push_own,
    push_role,
    gram_own,
    gram,
    iterates,
    mixing,
    dev_high,
    dev_low,
    centre_buf,
    result,
    load_sem,
    whole_sem,
    small_sem,
    ready_sem,
    halo_send,
    halo_recv,
    peer_send,
    peer_recv,
):
    n_member, n_domain, n_role, members = sizes
    rows = 64
    chunk = rows // n_member
    total = members * n_member
    slot_groups = 8 // n_role
    gram_rows = total // n_role
    groups = members // GROUP
    me_m = lax.axis_index("member")
    me_d = lax.axis_index("domain")
    me_r = lax.axis_index("role")

    def other(me, step, n):
        return lax.rem(me + (step + n), n)

    down, up = other(me_d, 1, n_domain), other(me_d, -1, n_domain)
    right, left = other(me_r, 1, n_role), other(me_r, -1, n_role)
    is_first, is_last = me_d == 0, me_d == n_domain - 1

    quarter = members * rows // 4
    loads = [
        pltpu.make_async_copy(
            ensemble_ref.at[k * quarter : (k + 1) * quarter], raw.at[k * quarter : (k + 1) * quarter], whole_sem.at[k]
        )
        for k in range(4)
    ]
    for copy in loads:
        copy.start()
    smalls = [
        pltpu.make_async_copy(src, dst, small_sem.at[k])
        for k, (src, dst) in enumerate(
            (
                (diffusion_hbm, diffusion_ref),
                (drift_rows_hbm, drift_rows_ref),
                (drift_cols_hbm, drift_cols_ref),
                (cells_hbm, cells_ref),
                (values_hbm, values_ref),
                (weights_hbm, weights_ref),
            )
        )
    ]
    for copy in smalls:
        copy.start()

    barrier = pltpu.get_barrier_semaphore()
    greeted = n_role - 1 + n_member - 1
    columns = (me_r, right, left)

    def greet(sem, domain):
        for r in columns:
            pl.semaphore_signal(sem, inc=1, device_id={"domain": domain, "role": r}, device_id_type=MESH)

    @pl.when(is_first)
    def _():
        greet(barrier, up)

    @pl.when(jnp.logical_not(is_last))
    def _():
        greet(barrier, down)

    for step in range(1, n_role):
        pl.semaphore_signal(barrier, inc=1, device_id={"role": other(me_r, step, n_role)}, device_id_type=MESH)
    for step in range(1, n_member):
        pl.semaphore_signal(barrier, inc=1, device_id={"member": other(me_m, step, n_member)}, device_id_type=MESH)

    lane = lax.broadcasted_iota(jnp.int32, (GROUP, LANES), 1)
    sub = lax.broadcasted_iota(jnp.int32, (GROUP, LANES), 0)
    seg_lane = lane
    for s in range(1, 6):
        seg_lane = jnp.where(lane >= SEG * s, lane - SEG * s, seg_lane)

    for copy in smalls + loads:
        copy.wait()

    def coef_row(row):
        diffusion = diffusion_ref[pl.ds(row, 1), :]
        drift_rows = drift_rows_ref[pl.ds(row, 1), :]
        drift_cols = drift_cols_ref[pl.ds(row, 1), :]
        keep = 1.0 - 4.0 * diffusion - drift_rows - drift_cols
        behind_row, behind_col = diffusion + drift_rows, diffusion + drift_cols
        return jnp.where(
            sub == 0, keep,
            jnp.where(sub == 1, diffusion, jnp.where(sub == 2, behind_row, behind_col)),
        )

    def turn(i, carry):
        for t in range(8):
            row = 8 * i + t
            field_a[row + 4, :members, :] = raw[pl.ds(row, members, stride=rows), :]
            field_a[row + 4, members:, :] = coef_row(row)
        return carry

    lax.fori_loop(0, rows // 8, turn, 0)
    top_rows[...] = field_a[4:8]
    bottom_rows[...] = field_a[rows : rows + 4]

    def stacked(pieces, masks):
        whole = pieces[0]
        for piece, mask in zip(pieces[1:], masks):
            whole = jnp.where(mask, piece, whole)
        return whole

    def turned(value, shift):
        return pltpu.roll(value, shift % LANES, value.ndim - 1) if shift % LANES else value

    strip_masks = [lane >= SEG * (k // 2) + 16 * (k % 2) for k in range(1, 2 * groups + 2)]
    quad_masks = [seg_lane >= 8, seg_lane >= 12, seg_lane >= 16]
    halo_mask = quad_masks[0] & (seg_lane < 16)
    seg_masks = [lane >= SEG * s for s in range(1, groups)]

    def own_strip(row):
        pieces = []
        for s in range(groups + 1):
            block = field_a[row, GROUP * s : GROUP * (s + 1), :]
            pieces += [turned(block, SEG * s + 8), turned(block, SEG * s + 16)]
        return stacked(pieces, strip_masks)

    def pack(q):
        own = [strip_a[4 + 4 * q + t] for t in range(4)]
        pack_right[q] = stacked([turned(own[t], 4 * t) for t in range(4)], quad_masks)
        pack_left[q] = stacked([turned(own[t], -4 * t) for t in range(3, -1, -1)], quad_masks)

    def own_strips(first, amount):
        for t in range(amount):
            strip_a[first + t] = own_strip(first + t)

    def own_block(i, carry):
        own_strips(8 + 14 * i, 14)
        return carry

    after_first = (me_d + n_domain - 1) // n_domain
    at_last = (me_d + 1) // n_domain
    pl.semaphore_wait(barrier, greeted + 3 * after_first + 3 * at_last)

    @pl.when(jnp.logical_not(is_first))
    def _():
        greet(ready_sem.at[0], up)

    @pl.when(is_last)
    def _():
        greet(ready_sem.at[1], down)

    def halo_copy(k, src, dst, where):
        return pltpu.make_async_remote_copy(
            src_ref=src, dst_ref=dst, send_sem=halo_send.at[k], recv_sem=halo_recv.at[k],
            device_id=where, device_id_type=MESH,
        )

    quads = rows // 4
    rows_down = halo_copy(0, bottom_rows, field_a.at[0:4], {"domain": down})
    rows_up = halo_copy(1, top_rows, field_a.at[rows + 4 : rows + 8], {"domain": up})
    sides = [
        halo_copy(2, pack_right, halo_left.at[1 : quads + 1], {"role": right}),
        halo_copy(3, pack_left, halo_right.at[1 : quads + 1], {"role": left}),
    ]
    corners_down = [
        halo_copy(4, pack_right.at[quads - 1], halo_left.at[0], {"domain": down, "role": right}),
        halo_copy(6, pack_left.at[quads - 1], halo_right.at[0], {"domain": down, "role": left}),
    ]
    corners_up = [
        halo_copy(5, pack_right.at[0], halo_left.at[quads + 1], {"domain": up, "role": right}),
        halo_copy(7, pack_left.at[0], halo_right.at[quads + 1], {"domain": up, "role": left}),
    ]

    @pl.when(jnp.logical_not(is_first))
    def _():
        rows_up.start()

    @pl.when(is_last)
    def _():
        rows_down.start()

    own_strips(4, 4)
    own_strips(rows, 4)
    pack(quads - 1)
    pack(0)

    @pl.when(is_last)
    def _():
        for copy in corners_down:
            copy.start()

    @pl.when(jnp.logical_not(is_first))
    def _():
        for copy in corners_up:
            copy.start()

    lax.fori_loop(0, 4, own_block, 0)
    for q in range(1, quads - 1):
        pack(q)
    for copy in sides:
        copy.start()

    def advanced(now, before, after, coef):
        axis = now.ndim - 1
        return (
            now * coef[0]
            + (after + pltpu.roll(now, LANES - 1, axis)) * coef[1]
            + before * coef[2]
            + pltpu.roll(now, 1, axis) * coef[3]
        )

    def field_coef(row):
        return [field_a[row, members + k : members + k + 1, :] for k in range(4)]

    def field_rows(source, target, shift, first, amount):
        before = source[first - 1, :members, :]
        now = source[first, :members, :]
        for i in range(amount):
            row = first + i
            after = source[row + 1, :members, :]
            target[row - shift, :members, :] = advanced(now, before, after, field_coef(row))
            before, now = now, after

    def seam_rows(source, first, amount):
        span, back, ahead = (slice(first + k, first + k + amount) for k in (0, -1, 1))
        coef = [strip_coef[span, k : k + 1, :] for k in range(4)]
        return advanced(source[span], source[back], source[ahead], coef)

    def merge(seam, first, amount):
        for i in range(amount):
            for s in range(groups):
                part = slice(GROUP * s, GROUP * (s + 1))
                begin = pltpu.roll(seam[i], (-(SEG * s + 16)) % LANES, 1)
                end = pltpu.roll(seam[i], (120 - SEG * s) % LANES, 1)
                block = final[first - 4 + i, part, :]
                final[first - 4 + i, part, :] = jnp.where(
                    lane < 4, begin, jnp.where(lane >= LANES - 4, end, block)
                )

    fields = (field_a, field_b, field_a, field_b, final)
    strips = (strip_a, strip_b, strip_a, strip_b)
    for step in range(STEPS):
        first, end = 5 + step, rows + 3 - step
        shift = 4 if step == STEPS - 1 else 0
        field_rows(fields[step], fields[step + 1], shift, first, end - first)

    @pl.when(jnp.logical_not(is_last))
    def _():
        pl.semaphore_wait(ready_sem.at[0], 3)
        rows_down.start()
        for copy in corners_down:
            copy.start()

    for copy in sides:
        copy.wait_recv()

    def unpack(q, carry):
        from_left = halo_left[q]
        from_right = halo_right[q]
        for t in range(4):
            row = 4 * q + t
            halo = jnp.where(quad_masks[1], turned(from_left, 8 - 4 * t), turned(from_right, 4 * t - 8))
            strip = jnp.where(halo_mask, halo, strip_a[row])
            strip_a[row] = strip
            strip_coef[row] = stacked([turned(strip, SEG * (s - groups)) for s in range(groups)], seg_masks)
        return carry

    lax.fori_loop(1, quads + 1, unpack, 0, unroll=4)

    for step in range(STEPS):
        first, end = 5 + step, rows + 3 - step
        while first < end:
            amount = min(31 if step < STEPS - 1 else 14, end - first)
            seam = seam_rows(strips[step], first, amount)
            if step < STEPS - 1:
                strips[step + 1][first : first + amount] = seam
            else:
                merge(seam, first, amount)
            first += amount

    def edge(first, last):
        for step in range(STEPS):
            shift = 4 if step == STEPS - 1 else 0
            begin = first + step if last else first - step
            field_rows(fields[step], fields[step + 1], shift, begin, 4)
            seam = seam_rows(strips[step], begin, 4)
            if step < STEPS - 1:
                strips[step + 1][begin : begin + 4] = seam
            else:
                merge(seam, begin, 4)

    rows_up.wait_recv()
    for copy in corners_up:
        copy.wait_recv()
    for t in range(4):
        strip_a[rows + 4 + t] = own_strip(rows + 4 + t)
    unpack(quads + 1, 0)
    edge(rows + 3, False)
    def peer_copy(stage, step, src, dst, axis):
        me, n = (me_m, n_member) if axis == "member" else (me_r, n_role)
        return pltpu.make_async_remote_copy(
            src_ref=src, dst_ref=dst, send_sem=peer_send.at[stage, step], recv_sem=peer_recv.at[stage, step],
            device_id={axis: other(me, step, n)}, device_id_type=MESH,
        )

    order = sorted(range(1, n_member), key=lambda s: -min(s, n_member - s))
    mine = pl.ds(pl.multiple_of(members * me_m, members), members)
    forward = {}
    for step in order:
        first = pl.multiple_of(chunk * other(me_m, step, n_member), chunk)
        forward[step] = peer_copy(0, step, final.at[pl.ds(first, chunk)], received.at[:, mine, :], "member")
    keep = pltpu.make_async_copy(
        final.at[pl.ds(pl.multiple_of(chunk * me_m, chunk), chunk)], received.at[:, mine, :], load_sem.at[1]
    )
    early = [s for s in order[::-1] if min(s, n_member - s) <= 2]
    late = [s for s in order if s not in early]

    def start_early(inner):
        for step in early:
            whom = other(me_m, step, n_member)
            ready = whom > 0

            @pl.when(ready if inner else jnp.logical_not(ready))
            def _(copy=forward[step]):
                copy.start()

    start_early(True)

    def observe(g, begin, end, seen):
        cell = cells_ref[pl.ds(g, 1), :]
        here = ((cell // LANES) % n_role) == me_r
        row_of = jnp.where(here, cell // (LANES * n_role), -1)
        row_of = jnp.broadcast_to(row_of, (members, LANES))
        col_of = jnp.broadcast_to(cell % LANES, (members, LANES))
        for row in range(begin, end):
            picked = jnp.take_along_axis(final[row], col_of, axis=1, mode="promise_in_bounds")
            seen = jnp.where(row_of == row, picked, seen)
        obs_part[g] = seen

    def observe_group(g, carry):
        for k in range(2):
            observe(2 * g + k, 4, rows, jnp.zeros((members, LANES), F32))
        return carry

    lax.fori_loop(0, 4, observe_group, 0)

    @pl.when(is_first)
    def _():
        pl.semaphore_wait(ready_sem.at[1], 3)
        rows_up.start()
        for copy in corners_up:
            copy.start()

    rows_down.wait_recv()
    for copy in corners_down:
        copy.wait_recv()
    for t in range(4):
        strip_a[t] = own_strip(t)
    unpack(0, 0)
    edge(1, True)
    start_early(False)

    def own_groups(r):
        return pl.ds(slot_groups * r, slot_groups)

    copies = []
    for step in list(range(1, n_role)) + [0]:
        whom = other(me_r, step, n_role)
        for k in range(slot_groups):
            g = slot_groups * whom + k
            observe(g, 0, 4, obs_part[g])
        if step:
            copies.append(peer_copy(1, step, obs_part.at[own_groups(whom)], obs_role.at[me_r], "role"))
            copies[-1].start()
    obs_role[me_r] = obs_part[own_groups(me_r)]
    for copy in copies:
        copy.wait()
    obs_own[...] = functools.reduce(jnp.add, [obs_role[r] for r in range(n_role)])

    copies = []
    for step in order:
        copies.append(peer_copy(2, step, obs_own, obs_all.at[:, mine, :], "member"))
        copies[-1].start()
    keep.start()
    obs_all[:, mine, :] = obs_own[...]
    for copy in copies:
        copy.wait()
    for step in late:
        forward[step].start()

    part = jnp.zeros((total, total), F32)
    push = jnp.zeros((GROUP, total), F32)
    slot = lax.broadcasted_iota(jnp.int32, (1, LANES), 1)
    for g in range(slot_groups):
        place = slot_groups * me_r + g
        observed = obs_all[g]
        centre = jnp.sum(observed, axis=0, keepdims=True) * (1.0 / total)
        deviation = observed - centre
        usable = slot + place * LANES < count_ref[0]
        weighted = deviation * jnp.where(usable, weights_ref[pl.ds(place, 1), :], 0.0)
        gap = jnp.broadcast_to(values_ref[pl.ds(place, 1), :] - centre, (GROUP, LANES))
        weighted = halves(weighted)
        part = part + product(halves(deviation), weighted, NT)
        push = push + product(halves(gap), weighted, NT)
    for r in range(n_role):
        gram_part[r] = part[gram_rows * r : gram_rows * (r + 1), :]
    push_own[...] = push[0:1, :]

    copies = []
    for step in range(1, n_role):
        copies.append(
            peer_copy(3, step, gram_part.at[other(me_r, step, n_role)], gram_role.at[me_r], "role")
        )
        copies[-1].start()
    pushes = []
    for step in range(1, n_role):
        pushes.append(peer_copy(6, step, push_own, push_role.at[me_r], "role"))
        pushes[-1].start()
    gram_role[me_r] = gram_part[me_r]
    push_role[me_r] = push_own[...]
    for copy in copies:
        copy.wait()
    gram_own[...] = functools.reduce(jnp.add, [gram_role[r] for r in range(n_role)])
    band = pl.ds(pl.multiple_of(gram_rows * me_r, gram_rows), gram_rows)
    copies = []
    for step in range(1, n_role):
        copies.append(peer_copy(4, step, gram_own, gram.at[band, :], "role"))
        copies[-1].start()
    gram[band, :] = gram_own[...]
    for copy in copies:
        copy.wait()

    across = lax.broadcasted_iota(jnp.int32, (total, total), 1)
    along = lax.broadcasted_iota(jnp.int32, (total, total), 0)
    diagonal = across == along
    matrix = gram[...] + jnp.where(diagonal, total - 1.0, 0.0)
    squares = jnp.sum(jnp.sum(matrix * matrix, axis=0, keepdims=True), axis=1, keepdims=True)
    scaling = jnp.sqrt(squares)
    scaled = matrix / scaling
    middle = jnp.where(diagonal, 1.5, 0.0) - 0.5 * scaled
    iterates[:total] = product(halves(scaled), halves(middle))
    iterates[total:] = middle

    def newton(i, carry):
        high, low = halves(iterates[...])
        inv, cur = (high[total:], low[total:]), (high[:total], low[:total])
        mid = halves(jnp.where(diagonal, 1.5, 0.0) - 0.5 * product(inv, cur))
        iterates[...] = product((high, low), mid)
        return carry

    lax.fori_loop(0, ITERS - 2, newton, 0)
    for copy in pushes:
        copy.wait()
    innovation = functools.reduce(jnp.add, [push_role[r] for r in range(n_role)])
    innovation = jnp.broadcast_to(innovation, (GROUP, total))
    inv = halves(iterates[total:])
    mid = halves(jnp.where(diagonal, 1.5, 0.0) - 0.5 * product(inv, halves(iterates[:total])))
    root = product(inv, mid)
    root_halves = halves(root)
    shifted = product(halves(product(halves(innovation), root_halves)), root_halves) / scaling
    mixing[...] = root * jnp.sqrt((total - 1.0) / scaling) + shifted[0:1, :]

    for step in order:
        forward[step].wait()
    keep.wait()
    for i in range(chunk):
        block = received[i]
        centre = jnp.sum(block, axis=0, keepdims=True) * (1.0 / total)
        high, low = halves(block - centre)
        span = slice(LANES * i, LANES * (i + 1))
        dev_high[:, span] = high
        dev_low[:, span] = low
        centre_buf[:, span] = centre

    back = []
    target_rows = pl.ds(pl.multiple_of(chunk * me_m, chunk), chunk)
    for step in order + [0]:
        first = pl.multiple_of(members * other(me_m, step, n_member), members)
        share = halves(mixing[pl.ds(first, members), :])
        updated = product(share, (dev_high[...], dev_low[...])) + centre_buf[...]
        for i in range(chunk):
            result[step, i] = updated[:, LANES * i : LANES * (i + 1)]
        if step:
            copy = peer_copy(5, step, result.at[step], out_ref.at[target_rows], "member")
        else:
            copy = pltpu.make_async_copy(result.at[step], out_ref.at[target_rows], load_sem.at[2])
        copy.start()
        back.append(copy)
    for copy in back[:-1]:
        copy.wait_send()
    for step in order[::-1]:
        back[order.index(step)].wait_recv()
    back[-1].wait()
    for copy in [rows_down, rows_up] + sides + corners_down + corners_up:
        copy.wait_send()


def shards(sizes, ensemble, diffusion, drift_rows, drift_cols, cells, count, values, weights):
    n_member, n_domain, n_role = sizes
    members, rows, cols = ensemble.shape
    total = members * n_member
    planes = members + GROUP
    chunk = rows // n_member
    slot_groups = 8 // n_role
    gram_rows = total // n_role

    def vmem(*shape, dtype=F32):
        return pltpu.VMEM(shape, dtype)

    packs = (rows // 4, GROUP, LANES)
    halos = (rows // 4 + 2, GROUP, LANES)
    out = pl.pallas_call(
        functools.partial(kernel, (n_member, n_domain, n_role, members)),
        name="forecast_analysis",
        out_shape=jax.ShapeDtypeStruct((rows, members, cols), F32),
        in_specs=[pl.BlockSpec(memory_space=pltpu.SMEM)] + [pl.BlockSpec(memory_space=pltpu.HBM)] * 7,
        out_specs=pl.BlockSpec(memory_space=pl.ANY),
        scratch_shapes=[
            vmem(members * rows, cols),
            vmem(rows, cols),
            vmem(rows, cols),
            vmem(rows, cols),
            vmem(8, LANES, dtype=jnp.int32),
            vmem(8, LANES),
            vmem(8, LANES),
            vmem(4, planes, cols),
            vmem(4, planes, cols),
            vmem(rows + 8, planes, cols),
            vmem(rows + 8, planes, cols),
            vmem(rows + 8, GROUP, LANES),
            vmem(rows + 8, GROUP, LANES),
            vmem(rows + 8, GROUP, LANES),
            vmem(*packs),
            vmem(*packs),
            vmem(*halos),
            vmem(*halos),
            vmem(rows, members, cols),
            vmem(chunk, total, cols),
            vmem(8, members, LANES),
            vmem(n_role, slot_groups, members, LANES),
            vmem(slot_groups, members, LANES),
            vmem(slot_groups, total, LANES),
            vmem(n_role, gram_rows, total),
            vmem(n_role, gram_rows, total),
            vmem(1, total),
            vmem(n_role, 1, total),
            vmem(gram_rows, total),
            vmem(total, total),
            vmem(2 * total, total),
            vmem(total, total),
            vmem(total, chunk * cols, dtype=BF16),
            vmem(total, chunk * cols, dtype=BF16),
            vmem(1, chunk * cols),
            vmem(n_member, chunk, members, cols),
            pltpu.SemaphoreType.DMA((3,)),
            pltpu.SemaphoreType.DMA((4,)),
            pltpu.SemaphoreType.DMA((6,)),
            pltpu.SemaphoreType.REGULAR((2,)),
            pltpu.SemaphoreType.DMA((8,)),
            pltpu.SemaphoreType.DMA((8,)),
            pltpu.SemaphoreType.DMA((7, 8)),
            pltpu.SemaphoreType.DMA((7, 8)),
        ],
        compiler_params=pltpu.CompilerParams(
            collective_id=0, has_side_effects=True, vmem_limit_bytes=40 << 20
        ),
    )(
        count,
        *(
            pltpu.with_memory_space_constraint(a, pltpu.HBM)
            for a in (
                ensemble.reshape(members * rows, cols),
                diffusion,
                drift_rows,
                drift_cols,
                cells.reshape(8, LANES),
                values.reshape(8, LANES),
                weights.reshape(8, LANES),
            )
        ),
    )
    return jnp.transpose(out, (1, 0, 2))


def solution(mesh):
    sizes = tuple(mesh.shape[a] for a in ("member", "domain", "role"))
    return jax.shard_map(
        functools.partial(shards, sizes),
        mesh=mesh,
        in_specs=(
            P("member", "domain", "role"),
            P("domain", "role"),
            P("domain", "role"),
            P("domain", "role"),
            P("domain", None),
            P("domain"),
            P("domain", None),
            P("domain", None),
        ),
        out_specs=P("member", "domain", "role"),
        check_vma=False,
    )
```
